32 devices in a mesh: group: 2 (over x), chan: 8 (over z, y), tm: 2 (over core).
Axes of the slice: x: 2, y: 2, z: 4, core: 2. Of those that a mesh axis runs over, the one named last changes fastest.
Arguments:
- signal: float32 [1664, 16384], P(('group', 'chan'), 'tm'), parts along dimension 0, may hold values from -56 to 56
- valid_flags: int32 [1664, 16], P(('group', 'chan'), 'tm'), parts along dimension 0, may hold values 0 or 1
Outputs:
- correlations: bfloat16 [2, 104, 1664, 512], P(None, 'tm', ('group', 'chan')), parts along dimension 2
The draws below stay inside these ranges and needn't reach their ends.
There are 2 independent parts, one for each index of `group`. The reference program is written for one: setup_inputs(seed, part) draws one part's arguments, and reference() takes and returns one part's arrays. A program takes and returns all parts, laid end to end along the dimension named above; each array names one. Nothing has to cross between parts.
All inputs are finite; a program needn't handle non-finite values. No bound on the sum of `valid_flags` on one device may be relied on, other than what follows from the above.
Results may differ from the reference program's by a relative error of at most 0.009.
Values may be sent and summed in bfloat16 or wider, within the bound.
No kernel may reach another device: no remote copies, remote signals or barrier semaphores. Data moves between devices by JAX's collectives and lax.ppermute only.
A program may use at most 192 MiB of HBM per device.

```python
import jax
import jax.numpy as jnp
from jax import lax

BLOCK = 104
WIN_DEV = 8
WINDOW = 1024
LAGS = 512
ROUNDS = 2
CHANNELS = 832
WINDOWS = 16
SAMPLES = 16384
N_CHAN = 8
N_TM = 2


def draw_signal(key, part):
    key_one, key_two, key_three, key_four = jax.random.split(key, 4)
    padded_length = SAMPLES + CHANNELS
    forward_wave = jax.random.truncated_normal(key_one, -4.0, 4.0, (padded_length,), jnp.float32)
    backward_wave = jax.random.truncated_normal(key_two, -4.0, 4.0, (padded_length,), jnp.float32)
    local_noise = jax.random.truncated_normal(key_three, -4.0, 4.0, (CHANNELS, SAMPLES), jnp.float32)
    window_gains = jnp.exp(jax.random.uniform(key_four, (CHANNELS, WINDOWS), jnp.float32, 0.0, 2.302585))

    def one_channel(channel_index):
        delay = channel_index // 2
        ahead_part = lax.dynamic_slice_in_dim(forward_wave, CHANNELS - delay, SAMPLES)
        behind = lax.dynamic_slice_in_dim(backward_wave, delay, SAMPLES)
        return ahead_part + behind
    coherent = lax.map(one_channel, jnp.arange(CHANNELS, dtype=jnp.int32))
    combined = 0.2 * coherent + local_noise
    scaled = combined.reshape(CHANNELS, WINDOWS, WINDOW) * window_gains[:, :, None]
    return scaled.reshape(CHANNELS, SAMPLES)


def plant(entries, own_key, least, high):
    dims = entries.shape
    spot = [jax.random.randint(jax.random.fold_in(own_key, axis), (), 0, dims[axis]) for axis in range(len(dims))]
    entries = entries.at[tuple(spot)].set(least)
    longest = dims.index(max(dims))
    spot[longest] = (spot[longest] + 1) % dims[longest]
    return entries.at[tuple(spot)].set(high)


def setup_inputs(seed: int = 0, part: int = 0) -> dict:
    streams_of = jax.random.split(jax.random.key(seed), 3)
    part_keys = jax.random.split(jax.random.fold_in(streams_of[2], part), 3)
    return {
        "signal": draw_signal(jax.random.fold_in(jax.random.fold_in(streams_of[2], part), 71), part),
        "valid_flags": plant((jax.random.randint(part_keys[1], (CHANNELS, WINDOWS), 0, 4) < 3).astype(jnp.int32), jax.random.fold_in(part_keys[1], 1), 0, 1),
    }


epsilon = 1e-06

def taper_table(window):
    sample_axis = jnp.arange(window, dtype=jnp.float32)
    return 0.5 - 0.5 * jnp.cos(2.0 * jnp.pi * sample_axis / window)

def forward_table(window):
    bin_count = window // 2
    sample_index = jnp.arange(window, dtype=jnp.int32)[:, None]
    frequency = jnp.arange(bin_count, dtype=jnp.int32)[None, :]
    phases = 2.0 * jnp.pi / window * (sample_index * frequency % window).astype(jnp.float32)
    return jnp.concatenate([jnp.cos(phases), -jnp.sin(phases)], axis=1).astype(jnp.bfloat16)

def lag_table(window, lag_count, windows):
    bin_count = window // 2
    frequency = jnp.arange(bin_count, dtype=jnp.int32)[:, None]
    shifts = jnp.arange(lag_count, dtype=jnp.int32)[None, :] - lag_count // 2
    phases = 2.0 * jnp.pi / window * (frequency * shifts % window).astype(jnp.float32)
    weight = jnp.where(frequency == 0, 1.0, 2.0).astype(jnp.float32) / (window * float(window * windows) ** 0.5)
    return jnp.concatenate([weight * jnp.cos(phases), -weight * jnp.sin(phases)], axis=0).astype(jnp.bfloat16)

def block_spectra(signal, valid_flags, window):
    row_count = signal.shape[0]
    window_count = signal.shape[1] // window
    pieces = signal.reshape(row_count, window_count, window).astype(jnp.float32)
    mean_square = lax.optimization_barrier(jnp.mean(pieces * pieces, axis=2, keepdims=True))
    tapered = (pieces * lax.rsqrt(mean_square + epsilon) * taper_table(window)).astype(jnp.bfloat16)
    spectra = jnp.dot(tapered.reshape(row_count * window_count, window), forward_table(window), preferred_element_type=jnp.float32)
    spectra = spectra.reshape(row_count, window_count, window) * valid_flags[:, :, None].astype(jnp.float32)
    return spectra.astype(jnp.bfloat16)

def cross_tile(partner, own_spectra):
    bin_count = partner.shape[2] // 2
    rotated = jnp.concatenate([-partner[:, :, bin_count:], partner[:, :, :bin_count]], axis=2)
    paired = jnp.stack([partner, rotated], axis=2).reshape(partner.shape[0], partner.shape[1], 2, 2, bin_count)
    halves = own_spectra.reshape(own_spectra.shape[0], own_spectra.shape[1], 2, bin_count)
    cross = jnp.einsum('dwjkf,cwkf->dcjf', paired.astype(jnp.float32), halves.astype(jnp.float32), precision=lax.Precision.HIGHEST)
    return cross.reshape(partner.shape[0], own_spectra.shape[0], 2 * bin_count)

def reference(signal, valid_flags):

    def spectra_of(pair_in):
        return block_spectra(pair_in[0], pair_in[1], WINDOW)
    spectra = lax.map(spectra_of, (signal.reshape(N_CHAN, BLOCK, SAMPLES), valid_flags.reshape(N_CHAN, BLOCK, WINDOWS)))
    lag_weights = lag_table(WINDOW, LAGS, WINDOWS)

    def one_block(pair_in):
        total = jnp.zeros((BLOCK, BLOCK, WINDOW), jnp.float32)
        for span in range(N_TM):
            partner_part = pair_in[0][:, span * WIN_DEV:(span + 1) * WIN_DEV]
            own_part = pair_in[1][:, span * WIN_DEV:(span + 1) * WIN_DEV]
            total = total + cross_tile(partner_part, own_part).astype(jnp.bfloat16).astype(jnp.float32)
        stacked = total.astype(jnp.bfloat16)
        lagged = jnp.dot(stacked.reshape(BLOCK * BLOCK, WINDOW), lag_weights, preferred_element_type=jnp.float32)
        return lagged.reshape(BLOCK, BLOCK, LAGS).astype(jnp.bfloat16)
    outputs = []
    for round_index in range(ROUNDS):
        partners = jnp.roll(spectra, -(round_index + 1), axis=0)
        tiles = lax.map(one_block, (partners, spectra))
        outputs.append(jnp.transpose(tiles, (1, 0, 2, 3)).reshape(BLOCK, CHANNELS, LAGS))
    return jnp.stack(outputs)
```

```python
import functools

import jax
import jax.numpy as jnp
import numpy as np
from jax import lax
from jax.experimental import pallas as pl
from jax.experimental.pallas import tpu as pltpu
from jax.sharding import PartitionSpec as P

WINDOW = 1024
LAGS = 512
ROUNDS = 2

epsilon = 1e-06

BINS = WINDOW // 2
HALF = BINS // 2
LANES = 128
GROUP = 8
OCTETS = BINS // GROUP
STEPS = OCTETS // 4
ROWS_PER_CHUNK = (20, 20, 12)

f32 = jnp.float32
bf16 = jnp.bfloat16


def frequency_order():
    order = np.zeros((OCTETS, GROUP), np.int64)
    for m in range(STEPS):
        for j in range(4):
            base = 16 * m + 8 * (j % 2) + np.arange(GROUP)
            order[4 * m + j] = base if j < 2 else np.where(base == 0, HALF, BINS - base)
    return order


def forward_rows():
    order = frequency_order()
    sample = np.arange(WINDOW)
    phases = 2.0 * np.pi / WINDOW * (order[:, :, None] * sample[None, None, :] % WINDOW)
    rows = np.stack([np.cos(phases), -np.sin(phases)], axis=1)
    return jnp.asarray(rows.reshape(WINDOW, WINDOW).astype(np.float32)).astype(bf16)


def lag_rows(windows):
    frequency = np.arange(HALF)
    weight = np.where(frequency == 0, 1.0, 2.0) / (WINDOW * float(WINDOW * windows) ** 0.5)
    tables = []
    for parity in range(2):
        shift = np.arange(parity, LAGS, 2)[:, None] - LAGS // 2
        phases = 2.0 * np.pi / WINDOW * (frequency[None, :] * shift % WINDOW)
        real = weight * np.cos(phases)
        imag = -weight * np.sin(phases)
        middle = 2.0 * np.pi / WINDOW * (HALF * shift[:, 0] % WINDOW)
        imag[:, 0] = weight[1] * (np.cos(middle) if parity == 0 else -np.sin(middle))
        tables.append(np.concatenate([real, imag], axis=1))
    return jnp.asarray(np.stack(tables).astype(np.float32)).astype(bf16)


def taper_row():
    return (0.5 - 0.5 * np.cos(2.0 * np.pi * np.arange(WINDOW) / WINDOW)).astype(np.float32)[None]


def spectra_kernel(chunks, half, me_ref, signal_ref, flags_ref, table_ref, taper_ref, *refs):
    outs, (tap, rows32) = refs[:-2], refs[-2:]
    piece_refs, own_ref = outs[:-1], outs[-1]
    row_count = signal_ref.shape[0]
    spans = signal_ref.shape[1] // WINDOW
    taper = taper_ref[...]
    tap[...] = jnp.zeros_like(tap)
    for w in range(spans):
        x = signal_ref[:, w * WINDOW : (w + 1) * WINDOW]
        mean_square = jnp.mean(x * x, axis=1, keepdims=True)
        scale = lax.rsqrt(mean_square + epsilon) * flags_ref[:, w : w + 1].astype(f32)
        tap[pl.ds(w * LANES, row_count), :] = (x * scale * taper).astype(bf16)
    for g in range(4):
        result = lax.dot_general(
            table_ref[g * 256 : (g + 1) * 256, :],
            tap[...],
            (((1,), (1,)), ((), ())),
            preferred_element_type=f32,
        )
        for o in range(16):
            position = g * 16 + o
            real = [result[o * 16 : o * 16 + 8, w * LANES : (w + 1) * LANES] for w in range(spans)]
            imag = [result[o * 16 + 8 : o * 16 + 16, w * LANES : (w + 1) * LANES] for w in range(spans)]
            plain = jnp.concatenate([p for w in range(spans) for p in (real[w], imag[w])], axis=0)
            turned = jnp.concatenate([p for w in range(spans) for p in (imag[w], -real[w])], axis=0)
            own_ref[position, :, :LANES] = plain.astype(bf16)
            own_ref[position, :, LANES:] = turned.astype(bf16)
            flipped = jnp.transpose(plain)
            for c in range(0, row_count, 8):
                rows32[pl.ds(c * OCTETS + position, 8, stride=OCTETS), :] = flipped[c : c + 8]
    me = me_ref[0]
    start = 0
    for k, rows in enumerate(chunks):
        for side in range(2):
            first = (me * half if side == 0 else (1 - me) * half) + start
            block = rows32[pl.ds(pl.multiple_of(first * OCTETS, OCTETS), rows * OCTETS), :]
            piece_refs[2 * k + side][...] = block.astype(bf16).reshape(rows, OCTETS, LANES)
        start += rows


def spectra(me, signal, valid_flags, table, taper, chunks, half):
    row_count = signal.shape[0]
    spans = signal.shape[1] // WINDOW
    pieces = [
        jax.ShapeDtypeStruct((rows, OCTETS, LANES), bf16) for rows in chunks for _ in range(2)
    ]
    own = jax.ShapeDtypeStruct((OCTETS, LANES, 2 * LANES), bf16)
    vmem = pl.BlockSpec(memory_space=pltpu.VMEM)
    return pl.pallas_call(
        functools.partial(spectra_kernel, chunks, half),
        out_shape=pieces + [own],
        in_specs=[pl.BlockSpec(memory_space=pltpu.SMEM)] + [vmem] * 4,
        out_specs=[vmem] * (len(pieces) + 1),
        scratch_shapes=[
            pltpu.VMEM((spans * LANES, WINDOW), bf16),
            pltpu.VMEM((row_count * OCTETS, LANES), f32),
        ],
        compiler_params=pltpu.CompilerParams(vmem_limit_bytes=60 << 20),
        cost_estimate=pl.CostEstimate(flops=2 * WINDOW**3, bytes_accessed=12 << 20, transcendentals=0),
        name="spectra",
    )(me, signal, valid_flags, table, taper)


def cross_kernel(parts, local_rows, row_count, has_prior, odd_ref, *refs):
    source_count = sum(2 * alternatives for _, _, _, alternatives in parts)
    near_ref, far_ref, lag_ref = refs[:3]
    sources = refs[3 : 3 + source_count]
    rest = refs[3 + source_count + (1 if has_prior else 0) :]
    out_ref, weights, packed, rows32, cross, mixed, result, in_sem, w_sem, out_sem = rest
    total = sum(part[2] for part in parts)
    pairs = total // 2

    weight_copies = []
    def w_copies(m):
        return [
            pltpu.make_async_copy(
                side.at[pl.ds(m * 4, 4)],
                weights.at[pl.ds(m * 4, 4), pl.ds(i * LANES, LANES), :],
                w_sem.at[i, m],
            )
            for i, side in enumerate((near_ref, far_ref))
        ]

    def load(part_index, side):
        cursor, row = 0, 0
        for index, (_, _, rows, alternatives) in enumerate(parts):
            if index == part_index:
                return [
                    pltpu.make_async_copy(
                        sources[cursor + 2 * a + side],
                        packed.at[pl.ds(row, rows), side],
                        in_sem.at[index, side],
                    )
                    for a in range(alternatives)
                ]
            cursor += 2 * alternatives
            row += rows

    for index, part in enumerate(parts):
        for side in range(2):
            copies = load(index, side)
            if len(copies) == 1:
                copies[0].start()
            else:
                odd = odd_ref[0]
                pl.when(odd == 0)(copies[0].start)
                pl.when(odd != 0)(copies[1].start)
    for m in range(STEPS):
        for copy in w_copies(m):
            copy.start()
    row = 0
    for index, part in enumerate(parts):
        for side in range(2):
            load(index, side)[0].wait()
        rows32[pl.ds(row, part[2])] = packed[pl.ds(row, part[2])].astype(f32)
        row += part[2]

    lane = lax.broadcasted_iota(jnp.int32, (GROUP, LANES), 1)
    sub = lax.broadcasted_iota(jnp.int32, (GROUP, LANES), 0)
    keep = lax.rem(lane, GROUP) == sub
    zero = jnp.zeros((GROUP, LANES), f32)
    top = sub == 0

    def step(m, first):
        for copy in w_copies(m):
            copy.wait()
        products = []
        for j in range(4):
            position = m * 4 + j
            blocks = []
            for d in range(total):
                halves = [
                    jnp.where(
                        keep,
                        jnp.broadcast_to(rows32[d, side, pl.ds(position, 1), :], (GROUP, LANES)),
                        zero,
                    )
                    for side in range(2)
                ]
                blocks.append(jnp.concatenate(halves, axis=1))
            left = jnp.concatenate(blocks, axis=0).astype(bf16)
            products.append(jnp.dot(left, weights[position], preferred_element_type=f32))
        base = pl.multiple_of(m * 16, 16)
        for d in range(total):
            a0, a1, b0, b1 = [p[d * GROUP : (d + 1) * GROUP] for p in products]
            s0, s1, t0, t1 = a0 + b0, a1 + b1, a0 - b0, a1 - b1
            even_real, odd_real = s0[:, :LANES], t0[:, :LANES]
            even_imag, odd_imag = t0[:, LANES:], s0[:, LANES:]
            if first:
                even_real = jnp.where(top, a0[:, :LANES], even_real)
                odd_real = jnp.where(top, a0[:, :LANES], odd_real)
                even_imag = jnp.where(top, b0[:, :LANES], even_imag)
                odd_imag = jnp.where(top, b0[:, LANES:], odd_imag)
            p, lanes = d // 2, pl.ds((d % 2) * LANES, LANES)
            for parity, offset, low, high in (
                (0, 0, even_real, s1[:, :LANES]),
                (0, HALF, even_imag, t1[:, LANES:]),
                (1, 0, odd_real, t1[:, :LANES]),
                (1, HALF, odd_imag, s1[:, LANES:]),
            ):
                cross[parity, p, pl.ds(base + offset, 16), lanes] = jnp.concatenate(
                    [low, high], axis=0
                ).astype(bf16)

    step(0, True)
    lax.fori_loop(1, STEPS, lambda m, c: (step(m, False), c)[1], 0)

    targets = [(part[0], part[1] + i) for part in parts for i in range(part[2])]
    out_copies = []
    for p in range(pairs):
        for parity in range(2):
            lagged = jnp.dot(lag_ref[parity], cross[parity, p], preferred_element_type=f32)
            for d in range(2):
                mixed[p % 2, d, pl.ds(parity, LAGS // 2, stride=2), :] = lagged[:, d * LANES : (d + 1) * LANES]
        for d in range(2):
            result[2 * p + d] = jnp.transpose(mixed[p % 2, d].astype(bf16))[:row_count]
            target = targets[2 * p + d]
            copy = pltpu.make_async_copy(
                result.at[2 * p + d], out_ref.at[target[0], target[1]], out_sem.at[2 * p + d]
            )
            copy.start()
            out_copies.append(copy)
    for copy in out_copies:
        copy.wait()


def cross_part(odd, near, far, lag_table, parts, sources, prior, local_rows, row_count):
    total = sum(part[2] for part in parts)
    any_space = pl.BlockSpec(memory_space=pl.ANY)
    operands = [odd, near, far, lag_table] + sources
    specs = [pl.BlockSpec(memory_space=pltpu.SMEM), any_space, any_space]
    specs += [pl.BlockSpec(memory_space=pltpu.VMEM)] + [any_space] * len(sources)
    aliases = {}
    if prior is not None:
        aliases = {len(operands): 0}
        operands.append(prior)
        specs.append(any_space)
    return pl.pallas_call(
        functools.partial(cross_kernel, tuple(parts), local_rows, row_count, prior is not None),
        out_shape=jax.ShapeDtypeStruct((ROUNDS, local_rows, row_count, LAGS), bf16),
        in_specs=specs,
        out_specs=any_space,
        scratch_shapes=[
            pltpu.VMEM((OCTETS, 2 * LANES, 2 * LANES), bf16),
            pltpu.VMEM((total, 2, OCTETS, LANES), bf16),
            pltpu.VMEM((total, 2, OCTETS, LANES), f32),
            pltpu.VMEM((2, total // 2, 2 * HALF, 2 * LANES), bf16),
            pltpu.VMEM((2, 2, LAGS, LANES), f32),
            pltpu.VMEM((total, row_count, LAGS), bf16),
            pltpu.SemaphoreType.DMA((len(parts), 2)),
            pltpu.SemaphoreType.DMA((2, STEPS)),
            pltpu.SemaphoreType.DMA((total,)),
        ],
        input_output_aliases=aliases,
        compiler_params=pltpu.CompilerParams(vmem_limit_bytes=60 << 20),
        cost_estimate=pl.CostEstimate(
            flops=total * 600_000_000 // 4, bytes_accessed=12 << 20, transcendentals=0
        ),
        name="cross",
    )(*operands)


def chunk_rows(local_rows):
    if sum(ROWS_PER_CHUNK) == local_rows:
        return ROWS_PER_CHUNK
    return (local_rows,)


def local(signal, valid_flags):
    row_count = signal.shape[0]
    span_windows = signal.shape[1] // WINDOW
    owner_count = lax.axis_size("tm")
    blocks = lax.axis_size("chan")
    local_rows = row_count // owner_count
    chunks = chunk_rows(local_rows)
    me = lax.axis_index("tm").astype(jnp.int32)
    odd = lax.rem(lax.axis_index("chan"), 2).astype(jnp.int32)

    *pieces, near = spectra(
        me[None], signal, valid_flags, forward_rows(), taper_row(), chunks, local_rows
    )
    pairs = lambda hops, cross: [
        (b * 2 + t, (b - hops) % blocks * 2 + (t if cross == 0 else 1 - t))
        for b in range(blocks)
        for t in range(2)
    ]
    axes = ("chan", "tm")
    two_away = [lax.ppermute(x, axes, pairs(2, i % 2)) for i, x in enumerate(pieces)]
    upward = [[q for q in pairs(1, side) if q[0] // 2 % 2 == 1] for side in range(2)]
    one_away = [lax.ppermute(x, axes, upward[i % 2]) for i, x in enumerate(pieces)]
    far = lax.ppermute(near, "tm", [(0, 1), (1, 0)])
    onward = [(b, b + 1) for b in range(0, blocks, 2)]
    relayed = [lax.ppermute(x, "chan", onward) for x in two_away]

    lag_table = lag_rows(span_windows * owner_count)
    out = None
    starts = np.cumsum([0] + list(chunks))
    for k in range(len(chunks) + 1):
        parts, sources = [], []
        if k < len(chunks):
            parts.append((1, int(starts[k]), chunks[k], 1))
            sources += two_away[2 * k : 2 * k + 2]
        if k > 0:
            parts.append((0, int(starts[k - 1]), chunks[k - 1], 2))
            sources += one_away[2 * k - 2 : 2 * k] + relayed[2 * k - 2 : 2 * k]
        out = cross_part(
            odd[None], near, far, lag_table, parts, sources, out, local_rows, row_count
        )
    return out


def solution(mesh):
    return jax.shard_map(
        local,
        mesh=mesh,
        in_specs=(P(("group", "chan"), "tm"), P(("group", "chan"), "tm")),
        out_specs=P(None, "tm", ("group", "chan"), None),
        check_vma=False,
    )
```

```python
import functools

import jax
import jax.numpy as jnp
import numpy as np
from jax import lax
from jax.experimental import pallas as pl
from jax.experimental.pallas import tpu as pltpu
from jax.sharding import PartitionSpec as P

WINDOW = 1024
LAGS = 512
ROUNDS = 2

epsilon = 1e-06

BINS = WINDOW // 2
HALF = BINS // 2
LANES = 128
GROUP = 8
OCTETS = BINS // GROUP
STEPS = OCTETS // 4
ROWS_PER_CHUNK = (20, 20, 12)

f32 = jnp.float32
bf16 = jnp.bfloat16


def frequency_order():
    order = np.zeros((OCTETS, GROUP), np.int64)
    for m in range(STEPS):
        for j in range(4):
            base = 16 * m + 8 * (j % 2) + np.arange(GROUP)
            order[4 * m + j] = base if j < 2 else np.where(base == 0, HALF, BINS - base)
    return order


def forward_rows():
    order = frequency_order()
    sample = np.arange(WINDOW)
    phases = 2.0 * np.pi / WINDOW * (order[:, :, None] * sample[None, None, :] % WINDOW)
    rows = np.stack([np.cos(phases), -np.sin(phases)], axis=1)
    return jnp.asarray(rows.reshape(WINDOW, WINDOW).astype(np.float32)).astype(bf16)


def lag_rows(windows):
    frequency = np.arange(HALF)
    weight = np.where(frequency == 0, 1.0, 2.0) / (WINDOW * float(WINDOW * windows) ** 0.5)
    tables = []
    for parity in range(2):
        shift = np.arange(parity, LAGS, 2)[:, None] - LAGS // 2
        phases = 2.0 * np.pi / WINDOW * (frequency[None, :] * shift % WINDOW)
        real = weight * np.cos(phases)
        imag = -weight * np.sin(phases)
        middle = 2.0 * np.pi / WINDOW * (HALF * shift[:, 0] % WINDOW)
        imag[:, 0] = weight[1] * (np.cos(middle) if parity == 0 else -np.sin(middle))
        tables.append(np.concatenate([real, imag], axis=1))
    return jnp.asarray(np.stack(tables).astype(np.float32)).astype(bf16)


def taper_row():
    return (0.5 - 0.5 * np.cos(2.0 * np.pi * np.arange(WINDOW) / WINDOW)).astype(np.float32)[None]


def spectra_kernel(chunks, half, me_ref, signal_ref, flags_ref, table_ref, taper_ref, *refs):
    outs, (tap, rows32, live) = refs[:-3], refs[-3:]
    piece_refs, own_ref = outs[:-1], outs[-1]
    row_count = signal_ref.shape[0]
    spans = signal_ref.shape[1] // WINDOW
    taper = taper_ref[...]
    tap[...] = jnp.zeros_like(tap)
    live[...] = jnp.zeros_like(live)
    live[:, :row_count] = flags_ref[...].astype(f32)
    for w in range(spans):
        x = signal_ref[:, w * WINDOW : (w + 1) * WINDOW]
        mean_square = jnp.mean(x * x, axis=1, keepdims=True)
        scale = lax.rsqrt(mean_square + epsilon)
        tap[pl.ds(w * LANES, row_count), :] = (x * scale * taper).astype(bf16)
    for g in range(4):
        result = lax.dot_general(
            table_ref[g * 256 : (g + 1) * 256, :],
            tap[...],
            (((1,), (1,)), ((), ())),
            preferred_element_type=f32,
        )
        for o in range(16):
            position = g * 16 + o
            tiles = [
                [
                    result[o * 16 + s * 8 : o * 16 + s * 8 + 8, w * LANES : (w + 1) * LANES]
                    * live[w : w + 1, :]
                    for w in range(spans)
                ]
                for s in range(2)
            ]
            real, imag = tiles
            plain = jnp.concatenate([p for w in range(spans) for p in (real[w], imag[w])], axis=0)
            turned = jnp.concatenate([p for w in range(spans) for p in (imag[w], -real[w])], axis=0)
            own_ref[position, :, :LANES] = plain.astype(bf16)
            own_ref[position, :, LANES:] = turned.astype(bf16)
            flipped = jnp.transpose(plain)
            for c in range(0, row_count, 8):
                rows32[pl.ds(c * OCTETS + position, 8, stride=OCTETS), :] = flipped[c : c + 8]
    me = me_ref[0]
    start = 0
    for k, rows in enumerate(chunks):
        for side in range(2):
            first = (me * half if side == 0 else (1 - me) * half) + start
            block = rows32[pl.ds(pl.multiple_of(first * OCTETS, OCTETS), rows * OCTETS), :]
            piece_refs[2 * k + side][...] = block.astype(bf16).reshape(rows, OCTETS, LANES)
        start += rows


def spectra(me, signal, valid_flags, table, taper, chunks, half):
    row_count = signal.shape[0]
    spans = signal.shape[1] // WINDOW
    pieces = [
        jax.ShapeDtypeStruct((rows, OCTETS, LANES), bf16)
        for rows in chunks
        for _ in range(2)
    ]
    own = jax.ShapeDtypeStruct((OCTETS, LANES, 2 * LANES), bf16)
    vmem = pl.BlockSpec(memory_space=pltpu.VMEM)
    return pl.pallas_call(
        functools.partial(spectra_kernel, chunks, half),
        out_shape=pieces + [own],
        in_specs=[pl.BlockSpec(memory_space=pltpu.SMEM)] + [vmem] * 4,
        out_specs=[vmem] * (len(pieces) + 1),
        scratch_shapes=[
            pltpu.VMEM((spans * LANES, WINDOW), bf16),
            pltpu.VMEM((row_count * OCTETS, LANES), f32),
            pltpu.VMEM((spans, LANES), f32),
        ],
        compiler_params=pltpu.CompilerParams(vmem_limit_bytes=60 << 20),
        cost_estimate=pl.CostEstimate(flops=2 * WINDOW**3, bytes_accessed=12 << 20, transcendentals=0),
        name="spectra",
    )(me, signal, valid_flags, table, taper)


def cross_kernel(parts, row_count, has_prior, odd_ref, *refs):
    source_count = sum(2 * alternatives for _, _, _, alternatives in parts)
    near_ref, far_ref, lag_ref = refs[:3]
    sources = refs[3 : 3 + source_count]
    rest = refs[3 + source_count + (1 if has_prior else 0) :]
    out_ref, packed, rows32, cross, mixed, result, in_sem, out_sem = rest
    total = sum(part[2] for part in parts)
    pairs = total // 2

    def load(part_index, side):
        cursor, row = 0, 0
        for index, (_, _, rows, alternatives) in enumerate(parts):
            if index == part_index:
                return [
                    pltpu.make_async_copy(
                        sources[cursor + 2 * a + side],
                        packed.at[pl.ds(row, rows), side],
                        in_sem.at[index, side],
                    )
                    for a in range(alternatives)
                ]
            cursor += 2 * alternatives
            row += rows

    for index, part in enumerate(parts):
        for side in range(2):
            copies = load(index, side)
            if len(copies) == 1:
                copies[0].start()
            else:
                odd = odd_ref[0]
                pl.when(odd == 0)(copies[0].start)
                pl.when(odd != 0)(copies[1].start)
    row = 0
    for index, part in enumerate(parts):
        for side in range(2):
            load(index, side)[0].wait()
        rows32[pl.ds(row, part[2])] = packed[pl.ds(row, part[2])].astype(f32)
        row += part[2]

    lane = lax.broadcasted_iota(jnp.int32, (GROUP, LANES), 1)
    sub = lax.broadcasted_iota(jnp.int32, (GROUP, LANES), 0)
    keep = lax.rem(lane, GROUP) == sub
    zero = jnp.zeros((GROUP, LANES), f32)
    top = sub == 0

    def step(m, first):
        products = []
        for j in range(4):
            position = m * 4 + j
            blocks = []
            for d in range(total):
                halves = [
                    jnp.where(
                        keep,
                        jnp.broadcast_to(rows32[d, side, pl.ds(position, 1), :], (GROUP, LANES)),
                        zero,
                    )
                    for side in range(2)
                ]
                blocks.append(jnp.concatenate(halves, axis=1))
            left = jnp.concatenate(blocks, axis=0).astype(bf16)
            weight = jnp.concatenate([near_ref[position], far_ref[position]], axis=0)
            products.append(jnp.dot(left, weight, preferred_element_type=f32))
        base = pl.multiple_of(m * 16, 16)
        for d in range(total):
            a0, a1, b0, b1 = [p[d * GROUP : (d + 1) * GROUP] for p in products]
            s0, s1, t0, t1 = a0 + b0, a1 + b1, a0 - b0, a1 - b1
            even_real, odd_real = s0[:, :LANES], t0[:, :LANES]
            even_imag, odd_imag = t0[:, LANES:], s0[:, LANES:]
            if first:
                even_real = jnp.where(top, a0[:, :LANES], even_real)
                odd_real = jnp.where(top, a0[:, :LANES], odd_real)
                even_imag = jnp.where(top, b0[:, :LANES], even_imag)
                odd_imag = jnp.where(top, b0[:, LANES:], odd_imag)
            p, lanes = d // 2, pl.ds((d % 2) * LANES, LANES)
            for parity, offset, low, high in (
                (0, 0, even_real, s1[:, :LANES]),
                (0, HALF, even_imag, t1[:, LANES:]),
                (1, 0, odd_real, t1[:, :LANES]),
                (1, HALF, odd_imag, s1[:, LANES:]),
            ):
                cross[parity, p, pl.ds(base + offset, 16), lanes] = jnp.concatenate(
                    [low, high], axis=0
                ).astype(bf16)

    step(0, True)
    lax.fori_loop(1, STEPS, lambda m, c: (step(m, False), c)[1], 0)

    targets = [(part[0], part[1] + i) for part in parts for i in range(part[2])]
    out_copies = []
    for p in range(pairs):
        for parity in range(2):
            lagged = jnp.dot(lag_ref[parity], cross[parity, p], preferred_element_type=f32)
            for d in range(2):
                mixed[p % 2, d, pl.ds(parity, LAGS // 2, stride=2), :] = lagged[:, d * LANES : (d + 1) * LANES]
        for d in range(2):
            result[2 * p + d] = jnp.transpose(mixed[p % 2, d].astype(bf16))[:row_count]
            target = targets[2 * p + d]
            copy = pltpu.make_async_copy(
                result.at[2 * p + d], out_ref.at[target[0], target[1]], out_sem.at[2 * p + d]
            )
            copy.start()
            out_copies.append(copy)
    for copy in out_copies:
        copy.wait()


def cross_part(odd, near, far, lag_table, parts, sources, prior, local_rows, row_count):
    total = sum(part[2] for part in parts)
    any_space = pl.BlockSpec(memory_space=pl.ANY)
    operands = [odd, near, far, lag_table] + sources
    specs = [pl.BlockSpec(memory_space=pltpu.SMEM)] + [pl.BlockSpec(memory_space=pltpu.VMEM)] * 3
    specs += [pl.BlockSpec(memory_space=pltpu.MemorySpace.HBM)] * len(sources)
    aliases = {}
    if prior is not None:
        aliases = {len(operands): 0}
        operands.append(prior)
        specs.append(any_space)
    return pl.pallas_call(
        functools.partial(cross_kernel, tuple(parts), row_count, prior is not None),
        out_shape=jax.ShapeDtypeStruct((ROUNDS, local_rows, row_count, LAGS), bf16),
        in_specs=specs,
        out_specs=any_space,
        scratch_shapes=[
            pltpu.VMEM((total, 2, OCTETS, LANES), bf16),
            pltpu.VMEM((total, 2, OCTETS, LANES), f32),
            pltpu.VMEM((2, total // 2, 2 * HALF, 2 * LANES), bf16),
            pltpu.VMEM((2, 2, LAGS, LANES), f32),
            pltpu.VMEM((total, row_count, LAGS), bf16),
            pltpu.SemaphoreType.DMA((len(parts), 2)),
            pltpu.SemaphoreType.DMA((total,)),
        ],
        input_output_aliases=aliases,
        compiler_params=pltpu.CompilerParams(vmem_limit_bytes=40 << 20),
        cost_estimate=pl.CostEstimate(
            flops=total * 600_000_000 // 4, bytes_accessed=12 << 20, transcendentals=0
        ),
        name="cross",
    )(*operands)


def chunk_rows(local_rows):
    if sum(ROWS_PER_CHUNK) == local_rows:
        return ROWS_PER_CHUNK
    return (local_rows,)


def local(signal, valid_flags):
    row_count = signal.shape[0]
    span_windows = signal.shape[1] // WINDOW
    owner_count = lax.axis_size("tm")
    blocks = lax.axis_size("chan")
    local_rows = row_count // owner_count
    chunks = chunk_rows(local_rows)
    me = lax.axis_index("tm").astype(jnp.int32)
    odd = lax.rem(lax.axis_index("chan"), 2).astype(jnp.int32)

    *pieces, near = spectra(
        me[None], signal, valid_flags.T, forward_rows(), taper_row(), chunks, local_rows
    )

    def back(hops, side):
        return [
            (b * owner_count + t, (b - hops) % blocks * owner_count + (t + side) % owner_count)
            for b in range(blocks)
            for t in range(owner_count)
        ]

    axes = ("chan", "tm")
    two_away = [lax.ppermute(x, axes, back(2, i % 2)) for i, x in enumerate(pieces)]
    one_away = [
        lax.ppermute(x, axes, [q for q in back(1, i % 2) if q[0] // owner_count % 2 == 1])
        for i, x in enumerate(pieces)
    ]
    far = lax.ppermute(near, "tm", [(0, 1), (1, 0)])
    onward = [(b, b + 1) for b in range(0, blocks, 2)]
    relayed = [lax.ppermute(x, "chan", onward) for x in two_away]

    lag_table = lag_rows(span_windows * owner_count)
    out = None
    starts = np.cumsum([0] + list(chunks))
    for k in range(len(chunks) + 1):
        parts, sources = [], []
        if k < len(chunks):
            parts.append((1, int(starts[k]), chunks[k], 1))
            sources += two_away[2 * k : 2 * k + 2]
        if k > 0:
            parts.append((0, int(starts[k - 1]), chunks[k - 1], 2))
            sources += one_away[2 * k - 2 : 2 * k] + relayed[2 * k - 2 : 2 * k]
        out = cross_part(
            odd[None], near, far, lag_table, parts, sources, out, local_rows, row_count
        )
    return out


def solution(mesh):
    return jax.shard_map(
        local,
        mesh=mesh,
        in_specs=(P(("group", "chan"), "tm"), P(("group", "chan"), "tm")),
        out_specs=P(None, "tm", ("group", "chan"), None),
        check_vma=False,
    )
```

```python
import functools

import jax
import jax.numpy as jnp
import numpy as np
from jax import lax
from jax.experimental import pallas as pl
from jax.experimental.pallas import tpu as pltpu
from jax.sharding import PartitionSpec as P

WINDOW = 1024
LAGS = 512
ROUNDS = 2

epsilon = 1e-06

BINS = WINDOW // 2
HALF = BINS // 2
LANES = 128
GROUP = 8
OCTETS = BINS // GROUP
STEPS = OCTETS // 4
ROWS_PER_CHUNK = (20, 20, 12)

f32 = jnp.float32
bf16 = jnp.bfloat16


def frequency_order():
    order = np.zeros((OCTETS, GROUP), np.int64)
    for m in range(STEPS):
        for j in range(4):
            base = 16 * m + 8 * (j % 2) + np.arange(GROUP)
            order[4 * m + j] = base if j < 2 else np.where(base == 0, HALF, BINS - base)
    return order


def forward_rows():
    order = frequency_order()
    sample = np.arange(WINDOW)
    phases = 2.0 * np.pi / WINDOW * (order[:, :, None] * sample[None, None, :] % WINDOW)
    rows = np.stack([np.cos(phases), -np.sin(phases)], axis=1)
    return jnp.asarray(rows.reshape(WINDOW, WINDOW).astype(np.float32)).astype(bf16)


def lag_rows(windows):
    frequency = np.arange(HALF)
    weight = np.where(frequency == 0, 1.0, 2.0) / (WINDOW * float(WINDOW * windows) ** 0.5)
    tables = []
    for parity in range(2):
        shift = np.arange(parity, LAGS, 2)[:, None] - LAGS // 2
        phases = 2.0 * np.pi / WINDOW * (frequency[None, :] * shift % WINDOW)
        real = weight * np.cos(phases)
        imag = -weight * np.sin(phases)
        middle = 2.0 * np.pi / WINDOW * (HALF * shift[:, 0] % WINDOW)
        imag[:, 0] = weight[1] * (np.cos(middle) if parity == 0 else -np.sin(middle))
        tables.append(np.concatenate([real, imag], axis=1))
    return jnp.asarray(np.stack(tables).astype(np.float32)).astype(bf16)


def taper_row():
    return (0.5 - 0.5 * np.cos(2.0 * np.pi * np.arange(WINDOW) / WINDOW)).astype(np.float32)[None]


def spectra_kernel(chunks, half, me_ref, signal_ref, flags_ref, table_ref, taper_ref, *refs):
    outs, (tap, rows32, live) = refs[:-3], refs[-3:]
    piece_refs, give_ref, own_ref = outs[:-2], outs[-2], outs[-1]
    row_count = signal_ref.shape[0]
    spans = signal_ref.shape[1] // WINDOW
    taper = taper_ref[...]
    tap[...] = jnp.zeros_like(tap)
    live[...] = jnp.zeros_like(live)
    live[:, :row_count] = flags_ref[...].astype(f32)
    for w in range(spans):
        x = signal_ref[:, w * WINDOW : (w + 1) * WINDOW]
        mean_square = jnp.mean(x * x, axis=1, keepdims=True)
        scale = lax.rsqrt(mean_square + epsilon)
        tap[pl.ds(w * LANES, row_count), :] = (x * scale * taper).astype(bf16)
    for g in range(4):
        result = lax.dot_general(
            table_ref[g * 256 : (g + 1) * 256, :],
            tap[...],
            (((1,), (1,)), ((), ())),
            preferred_element_type=f32,
        )
        for o in range(16):
            position = g * 16 + o
            tiles = [
                [
                    result[o * 16 + s * 8 : o * 16 + s * 8 + 8, w * LANES : (w + 1) * LANES]
                    * live[w : w + 1, :]
                    for w in range(spans)
                ]
                for s in range(2)
            ]
            real, imag = tiles
            plain = jnp.concatenate([p for w in range(spans) for p in (real[w], imag[w])], axis=0)
            turned = jnp.concatenate([p for w in range(spans) for p in (imag[w], -real[w])], axis=0)
            own_ref[position, :, :LANES] = plain.astype(bf16)
            own_ref[position, :, LANES:] = turned.astype(bf16)
            flipped = jnp.transpose(plain)
            for c in range(0, row_count, 8):
                rows32[pl.ds(c * OCTETS + position, 8, stride=OCTETS), :] = flipped[c : c + 8]
    me = me_ref[0]
    start = 0
    for k, rows in enumerate(chunks):
        for side in range(2):
            first = (me * half if side == 0 else (1 - me) * half) + start
            block = rows32[pl.ds(pl.multiple_of(first * OCTETS, OCTETS), rows * OCTETS), :]
            piece_refs[2 * k + side][...] = block.astype(bf16).reshape(rows, OCTETS, LANES)
        start += rows
    block = rows32[pl.ds(pl.multiple_of((1 - me) * half * OCTETS, OCTETS), half * OCTETS), :]
    give_ref[...] = block.astype(bf16).reshape(half, OCTETS, LANES)


def spectra(me, signal, valid_flags, table, taper, chunks, half):
    row_count = signal.shape[0]
    spans = signal.shape[1] // WINDOW
    pieces = [
        jax.ShapeDtypeStruct((rows, OCTETS, LANES), bf16)
        for rows in chunks
        for _ in range(2)
    ] + [jax.ShapeDtypeStruct((half, OCTETS, LANES), bf16)]
    own = jax.ShapeDtypeStruct((OCTETS, LANES, 2 * LANES), bf16)
    vmem = pl.BlockSpec(memory_space=pltpu.VMEM)
    return pl.pallas_call(
        functools.partial(spectra_kernel, chunks, half),
        out_shape=pieces + [own],
        in_specs=[pl.BlockSpec(memory_space=pltpu.SMEM)] + [vmem] * 4,
        out_specs=[vmem] * (len(pieces) + 1),
        scratch_shapes=[
            pltpu.VMEM((spans * LANES, WINDOW), bf16),
            pltpu.VMEM((row_count * OCTETS, LANES), f32),
            pltpu.VMEM((spans, LANES), f32),
        ],
        compiler_params=pltpu.CompilerParams(vmem_limit_bytes=60 << 20),
        cost_estimate=pl.CostEstimate(flops=2 * WINDOW**3, bytes_accessed=12 << 20, transcendentals=0),
        name="spectra",
    )(me, signal, valid_flags, table, taper)


def payload_kernel(first, rows, odd_ref, keep, taken, near_side, far_side, out_ref, hold, in_sem, out_sem):
    odd = odd_ref[0]
    span = pl.ds(first, rows)
    own = [pltpu.make_async_copy(keep, hold.at[0], in_sem.at[0]),
           pltpu.make_async_copy(taken.at[span], hold.at[1], in_sem.at[1])]
    come = [pltpu.make_async_copy(near_side, hold.at[0], in_sem.at[0]),
            pltpu.make_async_copy(far_side, hold.at[1], in_sem.at[1])]
    for i in range(2):
        pl.when(odd != 0)(own[i].start)
        pl.when(odd == 0)(come[i].start)
    leave = [pltpu.make_async_copy(hold.at[i], out_ref.at[i], out_sem.at[i]) for i in range(2)]
    for i in range(2):
        come[i].wait()
        leave[i].start()
    for i in range(2):
        leave[i].wait()


def payload(odd, keep, taken, near_side, far_side, first):
    hbm = pl.BlockSpec(memory_space=pltpu.MemorySpace.HBM)
    shape = (2,) + keep.shape
    return pl.pallas_call(
        functools.partial(payload_kernel, first, keep.shape[0]),
        out_shape=jax.ShapeDtypeStruct(shape, bf16),
        in_specs=[pl.BlockSpec(memory_space=pltpu.SMEM)] + [hbm] * 4,
        out_specs=hbm,
        scratch_shapes=[
            pltpu.VMEM(shape, bf16),
            pltpu.SemaphoreType.DMA((2,)),
            pltpu.SemaphoreType.DMA((2,)),
        ],
        compiler_params=pltpu.CompilerParams(vmem_limit_bytes=4 << 20),
        cost_estimate=pl.CostEstimate(flops=0, bytes_accessed=2 << 20, transcendentals=0),
        name="payload",
    )(odd, keep, taken, near_side, far_side)


def cross_kernel(parts, row_count, has_prior, *refs):
    source_count = sum(part[3] for part in parts)
    near_ref, far_ref, lag_ref = refs[:3]
    sources = refs[3 : 3 + source_count]
    rest = refs[3 + source_count + (1 if has_prior else 0) :]
    out_ref, packed, rows32, cross, mixed, result, in_sem, out_sem = rest
    total = sum(part[2] for part in parts)
    pairs = total // 2

    loads, cursor, row = [], 0, 0
    for index, (_, _, rows, arrays) in enumerate(parts):
        for side in range(2):
            source = sources[cursor].at[side] if arrays == 1 else sources[cursor + side]
            copy = pltpu.make_async_copy(
                source, packed.at[side, pl.ds(row, rows)], in_sem.at[index, side]
            )
            copy.start()
            loads.append((copy, side, row, rows))
        cursor += arrays
        row += rows
    for copy, side, row, rows in loads:
        copy.wait()
        rows32[side, pl.ds(row, rows)] = packed[side, pl.ds(row, rows)].astype(f32)

    lane = lax.broadcasted_iota(jnp.int32, (GROUP, LANES), 1)
    sub = lax.broadcasted_iota(jnp.int32, (GROUP, LANES), 0)
    keep = lax.rem(lane, GROUP) == sub
    zero = jnp.zeros((GROUP, LANES), f32)
    top = sub == 0

    def step(m, first):
        products = []
        for j in range(4):
            position = m * 4 + j
            blocks = []
            for d in range(total):
                halves = [
                    jnp.where(
                        keep,
                        jnp.broadcast_to(rows32[side, d, pl.ds(position, 1), :], (GROUP, LANES)),
                        zero,
                    )
                    for side in range(2)
                ]
                blocks.append(jnp.concatenate(halves, axis=1))
            left = jnp.concatenate(blocks, axis=0).astype(bf16)
            weight = jnp.concatenate([near_ref[position], far_ref[position]], axis=0)
            products.append(jnp.dot(left, weight, preferred_element_type=f32))
        base = pl.multiple_of(m * 16, 16)
        for d in range(total):
            a0, a1, b0, b1 = [p[d * GROUP : (d + 1) * GROUP] for p in products]
            s0, s1, t0, t1 = a0 + b0, a1 + b1, a0 - b0, a1 - b1
            even_real, odd_real = s0[:, :LANES], t0[:, :LANES]
            even_imag, odd_imag = t0[:, LANES:], s0[:, LANES:]
            if first:
                even_real = jnp.where(top, a0[:, :LANES], even_real)
                odd_real = jnp.where(top, a0[:, :LANES], odd_real)
                even_imag = jnp.where(top, b0[:, :LANES], even_imag)
                odd_imag = jnp.where(top, b0[:, LANES:], odd_imag)
            p, lanes = d // 2, pl.ds((d % 2) * LANES, LANES)
            for parity, offset, low, high in (
                (0, 0, even_real, s1[:, :LANES]),
                (0, HALF, even_imag, t1[:, LANES:]),
                (1, 0, odd_real, t1[:, :LANES]),
                (1, HALF, odd_imag, s1[:, LANES:]),
            ):
                cross[parity, p, pl.ds(base + offset, 16), lanes] = jnp.concatenate(
                    [low, high], axis=0
                ).astype(bf16)

    step(0, True)
    lax.fori_loop(1, STEPS, lambda m, c: (step(m, False), c)[1], 0)

    targets = [(part[0], part[1] + i) for part in parts for i in range(part[2])]
    out_copies = []
    for p in range(pairs):
        for parity in range(2):
            lagged = jnp.dot(lag_ref[parity], cross[parity, p], preferred_element_type=f32)
            for d in range(2):
                mixed[p % 2, d, pl.ds(parity, LAGS // 2, stride=2), :] = lagged[:, d * LANES : (d + 1) * LANES]
        for d in range(2):
            result[2 * p + d] = jnp.transpose(mixed[p % 2, d].astype(bf16))[:row_count]
            target = targets[2 * p + d]
            copy = pltpu.make_async_copy(
                result.at[2 * p + d], out_ref.at[target[0], target[1]], out_sem.at[2 * p + d]
            )
            copy.start()
            out_copies.append(copy)
    for copy in out_copies:
        copy.wait()


def cross_part(near, far, lag_table, parts, sources, prior, local_rows, row_count):
    total = sum(part[2] for part in parts)
    any_space = pl.BlockSpec(memory_space=pl.ANY)
    operands = [near, far, lag_table] + sources
    specs = [pl.BlockSpec(memory_space=pltpu.VMEM)] * 3
    specs += [pl.BlockSpec(memory_space=pltpu.MemorySpace.HBM)] * len(sources)
    aliases = {}
    if prior is not None:
        aliases = {len(operands): 0}
        operands.append(prior)
        specs.append(any_space)
    return pl.pallas_call(
        functools.partial(cross_kernel, tuple(parts), row_count, prior is not None),
        out_shape=jax.ShapeDtypeStruct((ROUNDS, local_rows, row_count, LAGS), bf16),
        in_specs=specs,
        out_specs=any_space,
        scratch_shapes=[
            pltpu.VMEM((2, total, OCTETS, LANES), bf16),
            pltpu.VMEM((2, total, OCTETS, LANES), f32),
            pltpu.VMEM((2, total // 2, 2 * HALF, 2 * LANES), bf16),
            pltpu.VMEM((2, 2, LAGS, LANES), f32),
            pltpu.VMEM((total, row_count, LAGS), bf16),
            pltpu.SemaphoreType.DMA((len(parts), 2)),
            pltpu.SemaphoreType.DMA((total,)),
        ],
        input_output_aliases=aliases,
        compiler_params=pltpu.CompilerParams(vmem_limit_bytes=32 << 20),
        cost_estimate=pl.CostEstimate(
            flops=total * 600_000_000 // 4, bytes_accessed=12 << 20, transcendentals=0
        ),
        name="cross",
    )(*operands)


def chunk_rows(local_rows):
    if sum(ROWS_PER_CHUNK) == local_rows:
        return ROWS_PER_CHUNK
    return (local_rows,)


def local(signal, valid_flags):
    row_count = signal.shape[0]
    span_windows = signal.shape[1] // WINDOW
    owner_count = lax.axis_size("tm")
    blocks = lax.axis_size("chan")
    local_rows = row_count // owner_count
    chunks = chunk_rows(local_rows)
    me = lax.axis_index("tm").astype(jnp.int32)
    odd = lax.rem(lax.axis_index("chan"), 2).astype(jnp.int32)

    *pieces, give, near = spectra(
        me[None], signal, valid_flags.T, forward_rows(), taper_row(), chunks, local_rows
    )

    def back(hops, side):
        return [
            (b * owner_count + t, (b - hops) % blocks * owner_count + (t + side) % owner_count)
            for b in range(blocks)
            for t in range(owner_count)
        ]

    axes = ("chan", "tm")
    two_away = [lax.ppermute(x, axes, back(2, i % 2)) for i, x in enumerate(pieces)]
    other = [(t, 1 - t) for t in range(owner_count)]
    taken = lax.ppermute(give, "tm", other)
    far = lax.ppermute(near, "tm", other)
    swap = [(b, b - 1 if b % 2 else b + 1) for b in range(blocks)]

    lag_table = lag_rows(span_windows * owner_count)
    out = None
    starts = np.cumsum([0] + list(chunks))
    one_away = []
    for k in range(len(chunks) + 1):
        parts, sources = [], []
        if k < len(chunks):
            sent = two_away[2 * k : 2 * k + 2]
            load = payload(odd[None], pieces[2 * k], taken, *sent, int(starts[k]))
            one_away.append(lax.ppermute(load, "chan", swap))
            parts.append((1, int(starts[k]), chunks[k], 2))
            sources += sent
        if k > 0:
            parts.append((0, int(starts[k - 1]), chunks[k - 1], 1))
            sources.append(one_away[k - 1])
        out = cross_part(near, far, lag_table, parts, sources, out, local_rows, row_count)
    return out


def solution(mesh):
    return jax.shard_map(
        local,
        mesh=mesh,
        in_specs=(P(("group", "chan"), "tm"), P(("group", "chan"), "tm")),
        out_specs=P(None, "tm", ("group", "chan"), None),
        check_vma=False,
    )
```

```python
import functools

import jax
import jax.numpy as jnp
import numpy as np
from jax import lax
from jax.experimental import pallas as pl
from jax.experimental.pallas import tpu as pltpu
from jax.sharding import PartitionSpec as P

WINDOW = 1024
LAGS = 512
ROUNDS = 2

epsilon = 1e-06

BINS = WINDOW // 2
HALF = BINS // 2
LANES = 128
GROUP = 8
OCTETS = BINS // GROUP
STEPS = OCTETS // 4
ROWS_PER_CHUNK = (14, 14, 12, 12)

f32 = jnp.float32
bf16 = jnp.bfloat16


def frequency_order():
    order = np.zeros((OCTETS, GROUP), np.int64)
    for m in range(STEPS):
        for j in range(4):
            base = 16 * m + 8 * (j % 2) + np.arange(GROUP)
            order[4 * m + j] = base if j < 2 else np.where(base == 0, HALF, BINS - base)
    return order


def forward_rows():
    order = frequency_order()
    sample = np.arange(WINDOW)
    phases = 2.0 * np.pi / WINDOW * (order[:, :, None] * sample[None, None, :] % WINDOW)
    rows = np.stack([np.cos(phases), -np.sin(phases)], axis=1)
    return jnp.asarray(rows.reshape(WINDOW, WINDOW).astype(np.float32)).astype(bf16)


def lag_rows(windows):
    frequency = np.arange(HALF)
    weight = np.where(frequency == 0, 1.0, 2.0) / (WINDOW * float(WINDOW * windows) ** 0.5)
    tables = []
    for parity in range(2):
        shift = np.arange(parity, LAGS, 2)[:, None] - LAGS // 2
        phases = 2.0 * np.pi / WINDOW * (frequency[None, :] * shift % WINDOW)
        real = weight * np.cos(phases)
        imag = -weight * np.sin(phases)
        middle = 2.0 * np.pi / WINDOW * (HALF * shift[:, 0] % WINDOW)
        imag[:, 0] = weight[1] * (np.cos(middle) if parity == 0 else -np.sin(middle))
        tables.append(np.concatenate([real, imag], axis=1))
    return jnp.asarray(np.stack(tables).astype(np.float32)).astype(bf16)


def taper_row():
    return (0.5 - 0.5 * np.cos(2.0 * np.pi * np.arange(WINDOW) / WINDOW)).astype(np.float32)[None]


def window_order(spans):
    return [w for start in range(2) for w in range(start, spans, 2)]


def table_copies(table_hbm, table, sem):
    return [
        pltpu.make_async_copy(
            table_hbm.at[pl.ds(g * 256, 256)], table.at[pl.ds(g * 256, 256)], sem.at[g]
        )
        for g in range(4)
    ]


def taper_rows(x, taper):
    mean_square = jnp.mean(x * x, axis=1, keepdims=True)
    return (x * lax.rsqrt(mean_square + epsilon) * taper).astype(bf16)


def transform(table, tap, g):
    return lax.dot_general(
        table[g * 256 : (g + 1) * 256, :],
        tap[...],
        (((1,), (1,)), ((), ())),
        preferred_element_type=f32,
    )


def first_kernel(
    rows, half, bounds, me_ref, signal_hbm, live_ref, table_hbm, taper_ref,
    same_ref, cross_ref, signal, tap, table, rows32, in_sem, table_sem,
):
    spans = signal.shape[1] // WINDOW
    width = LANES // 2
    loads, held = [], 0
    for h, (low, high) in enumerate(bounds):
        copy = pltpu.make_async_copy(
            signal_hbm.at[pl.ds(low, high - low)], signal.at[pl.ds(held, high - low)], in_sem.at[h]
        )
        copy.start()
        loads.append(copy)
        held += high - low
    tables = table_copies(table_hbm, table, table_sem)
    for copy in tables:
        copy.start()
    taper = taper_ref[...]
    tap[...] = jnp.zeros_like(tap)
    for copy in loads:
        copy.wait()
    for w in range(spans):
        x = signal[:, w * WINDOW : (w + 1) * WINDOW]
        tap[pl.ds(w * width, held), :] = taper_rows(x, taper)
    for g in range(4):
        tables[g].wait()
        result = transform(table, tap, g)
        for o in range(16):
            position = g * 16 + o
            plain = jnp.concatenate(
                [
                    result[o * 16 : o * 16 + 16, v * LANES : (v + 1) * LANES] * live_ref[v : v + 1, :]
                    for v in range(spans // 2)
                ],
                axis=0,
            )
            flipped = jnp.transpose(plain)
            for c in range(0, held, 8):
                rows32[pl.ds(c * OCTETS + position, 8, stride=OCTETS), :] = jnp.concatenate(
                    [flipped[c : c + 8], flipped[width + c : width + c + 8]], axis=1
                )
    me = me_ref[0]
    places = (-bounds[0][0], bounds[0][1] - bounds[0][0] + half - bounds[1][0])
    for side, out in enumerate((same_ref, cross_ref)):
        place = jnp.where(me == side, places[0], places[1])
        block = rows32[pl.ds(pl.multiple_of(place * OCTETS, OCTETS), rows * OCTETS), :]
        out[...] = block.astype(bf16).reshape(rows, OCTETS, LANES)


def first_flags(flags, rows, half):
    width = LANES // 2
    parts = [flags[:, h * half // 8 * 8 : -(-(h * half + rows) // 8) * 8] for h in range(2)]
    held = jnp.concatenate(parts, axis=1)
    held = jnp.pad(held, ((0, 0), (0, width - held.shape[1])))
    return held.reshape(flags.shape[0] // 2, LANES)


def first_spectra(me, signal, live, table, taper, rows, half):
    spans = signal.shape[1] // WINDOW
    bounds = []
    for h in range(2):
        bounds.append((h * half // 8 * 8, -(-(h * half + rows) // 8) * 8))
    held = sum(high - low for low, high in bounds)
    assert held <= LANES // 2
    vmem = pl.BlockSpec(memory_space=pltpu.VMEM)
    hbm = pl.BlockSpec(memory_space=pltpu.MemorySpace.HBM)
    return pl.pallas_call(
        functools.partial(first_kernel, rows, half, tuple(bounds)),
        out_shape=[jax.ShapeDtypeStruct((rows, OCTETS, LANES), bf16)] * 2,
        in_specs=[pl.BlockSpec(memory_space=pltpu.SMEM), hbm, vmem, hbm, vmem],
        out_specs=[vmem] * 2,
        scratch_shapes=[
            pltpu.VMEM((held, spans * WINDOW), f32),
            pltpu.VMEM((spans * LANES // 2, WINDOW), bf16),
            pltpu.VMEM((WINDOW, WINDOW), bf16),
            pltpu.VMEM((held * OCTETS, LANES), f32),
            pltpu.SemaphoreType.DMA((2,)),
            pltpu.SemaphoreType.DMA((4,)),
        ],
        compiler_params=pltpu.CompilerParams(vmem_limit_bytes=32 << 20),
        cost_estimate=pl.CostEstimate(flops=WINDOW**3, bytes_accessed=6 << 20, transcendentals=0),
        name="first",
    )(me, signal, live, table, taper)


def spectra_kernel(
    chunks, half, me_ref, signal_hbm, flags_ref, table_hbm, taper_ref, *refs
):
    count = 2 * len(chunks) - 2
    pieces, (give_hbm, own_hbm) = refs[:count], refs[count : count + 2]
    signal, tap, table, rows32, live, own, give, in_sem, table_sem, own_sem, give_sem = refs[count + 2 :]
    row_count = signal.shape[0]
    spans = signal.shape[1] // WINDOW
    loads = []
    for w in range(spans):
        part = pl.ds(w * WINDOW, WINDOW)
        copy = pltpu.make_async_copy(signal_hbm.at[:, part], signal.at[:, part], in_sem.at[w])
        copy.start()
        loads.append(copy)
    tables = table_copies(table_hbm, table, table_sem)
    for copy in tables:
        copy.start()
    taper = taper_ref[...]
    tap[...] = jnp.zeros_like(tap)
    live[...] = jnp.zeros_like(live)
    live[:, :row_count] = flags_ref[...].astype(f32)
    for w in range(spans):
        loads[w].wait()
        x = signal[:, w * WINDOW : (w + 1) * WINDOW]
        tap[pl.ds(w * LANES, row_count), :] = taper_rows(x, taper)
    order = window_order(spans)
    leaving = []
    for g in range(4):
        tables[g].wait()
        result = transform(table, tap, g)
        for o in range(16):
            position = g * 16 + o
            real, imag = [
                [
                    result[o * 16 + s * 8 : o * 16 + s * 8 + 8, w * LANES : (w + 1) * LANES]
                    * live[w : w + 1, :]
                    for w in order
                ]
                for s in range(2)
            ]
            plain = jnp.concatenate([p for pair in zip(real, imag) for p in pair], axis=0)
            turned = jnp.concatenate([p for r, i in zip(real, imag) for p in (i, -r)], axis=0)
            own[position, :, :LANES] = plain.astype(bf16)
            own[position, :, LANES:] = turned.astype(bf16)
            flipped = jnp.transpose(plain)
            for c in range(0, row_count, 8):
                rows32[pl.ds(c * OCTETS + position, 8, stride=OCTETS), :] = flipped[c : c + 8]
        part = pl.ds(g * 16, 16)
        leaving.append(pltpu.make_async_copy(own.at[part], own_hbm.at[part], own_sem.at[g]))
        leaving[-1].start()
    me = me_ref[0]

    def block(side, start, rows):
        first = (me * half if side == 0 else (1 - me) * half) + start
        value = rows32[pl.ds(pl.multiple_of(first * OCTETS, OCTETS), rows * OCTETS), :]
        return value.astype(bf16).reshape(rows, OCTETS, LANES)

    give[...] = block(1, 0, half)
    leaving.append(pltpu.make_async_copy(give, give_hbm, give_sem))
    leaving[-1].start()
    start = chunks[0]
    for k, rows in enumerate(chunks[1:]):
        for side in range(2):
            pieces[2 * k + side][...] = block(side, start, rows)
        start += rows
    for copy in leaving:
        copy.wait()


def spectra(me, signal, flags, table, taper, chunks, half):
    row_count = signal.shape[0]
    spans = signal.shape[1] // WINDOW
    shapes = [(rows, OCTETS, LANES) for rows in chunks[1:] for _ in range(2)]
    give, own = (half, OCTETS, LANES), (OCTETS, LANES, 2 * LANES)
    vmem = pl.BlockSpec(memory_space=pltpu.VMEM)
    hbm = pl.BlockSpec(memory_space=pltpu.MemorySpace.HBM)
    return pl.pallas_call(
        functools.partial(spectra_kernel, chunks, half),
        out_shape=[jax.ShapeDtypeStruct(shape, bf16) for shape in shapes + [give, own]],
        in_specs=[pl.BlockSpec(memory_space=pltpu.SMEM), hbm, vmem, hbm, vmem],
        out_specs=[vmem] * len(shapes) + [hbm] * 2,
        scratch_shapes=[
            pltpu.VMEM((row_count, spans * WINDOW), f32),
            pltpu.VMEM((spans * LANES, WINDOW), bf16),
            pltpu.VMEM((WINDOW, WINDOW), bf16),
            pltpu.VMEM((row_count * OCTETS, LANES), f32),
            pltpu.VMEM((spans, LANES), f32),
            pltpu.VMEM(own, bf16),
            pltpu.VMEM(give, bf16),
            pltpu.SemaphoreType.DMA((spans,)),
            pltpu.SemaphoreType.DMA((4,)),
            pltpu.SemaphoreType.DMA((4,)),
            pltpu.SemaphoreType.DMA,
        ],
        compiler_params=pltpu.CompilerParams(vmem_limit_bytes=40 << 20),
        cost_estimate=pl.CostEstimate(flops=2 * WINDOW**3, bytes_accessed=12 << 20, transcendentals=0),
        name="spectra",
    )(me, signal, flags, table, taper)


def payload_kernel(first, rows, odd_ref, keep, taken, near_side, far_side, out_ref, hold, in_sem, out_sem):
    odd = odd_ref[0]
    span = pl.ds(first, rows)
    own = [pltpu.make_async_copy(keep, hold.at[0], in_sem.at[0]),
           pltpu.make_async_copy(taken.at[span], hold.at[1], in_sem.at[1])]
    come = [pltpu.make_async_copy(near_side, hold.at[0], in_sem.at[0]),
            pltpu.make_async_copy(far_side, hold.at[1], in_sem.at[1])]
    for i in range(2):
        pl.when(odd != 0)(own[i].start)
        pl.when(odd == 0)(come[i].start)
    leave = [pltpu.make_async_copy(hold.at[i], out_ref.at[i], out_sem.at[i]) for i in range(2)]
    for i in range(2):
        come[i].wait()
        leave[i].start()
    for i in range(2):
        leave[i].wait()


def payload(odd, keep, taken, near_side, far_side, first):
    hbm = pl.BlockSpec(memory_space=pltpu.MemorySpace.HBM)
    shape = (2,) + keep.shape
    return pl.pallas_call(
        functools.partial(payload_kernel, first, keep.shape[0]),
        out_shape=jax.ShapeDtypeStruct(shape, bf16),
        in_specs=[pl.BlockSpec(memory_space=pltpu.SMEM)] + [hbm] * 4,
        out_specs=hbm,
        scratch_shapes=[
            pltpu.VMEM(shape, bf16),
            pltpu.SemaphoreType.DMA((2,)),
            pltpu.SemaphoreType.DMA((2,)),
        ],
        compiler_params=pltpu.CompilerParams(vmem_limit_bytes=4 << 20),
        cost_estimate=pl.CostEstimate(flops=0, bytes_accessed=2 << 20, transcendentals=0),
        name="payload",
    )(odd, keep, taken, near_side, far_side)


def cross_kernel(parts, row_count, has_prior, *refs):
    source_count = sum(part[3] for part in parts)
    near_ref, far_hbm, lag_hbm = refs[:3]
    sources = refs[3 : 3 + source_count]
    rest = refs[3 + source_count + (1 if has_prior else 0) :]
    out_ref, far_ref, lag_ref, packed, rows32, cross, mixed, result = rest[:8]
    in_sem, far_sem, lag_sem, out_sem = rest[8:]
    total = sum(part[2] for part in parts)
    pairs = total // 2

    loads, cursor, row = [], 0, 0
    for index, (_, _, rows, arrays) in enumerate(parts):
        for side in range(2):
            source = sources[cursor].at[side] if arrays == 1 else sources[cursor + side]
            copy = pltpu.make_async_copy(
                source, packed.at[side, pl.ds(row, rows)], in_sem.at[index, side]
            )
            copy.start()
            loads.append((copy, side, row, rows))
        cursor += arrays
        row += rows

    def far_copy(m):
        part = pl.ds(m * 4, 4)
        return pltpu.make_async_copy(far_hbm.at[part], far_ref.at[part], far_sem.at[m])

    for m in range(STEPS):
        far_copy(m).start()
    lag_copy = pltpu.make_async_copy(lag_hbm, lag_ref, lag_sem)
    lag_copy.start()
    for copy, side, row, rows in loads:
        copy.wait()
        rows32[side, pl.ds(row, rows)] = packed[side, pl.ds(row, rows)].astype(f32)

    lane = lax.broadcasted_iota(jnp.int32, (GROUP, LANES), 1)
    sub = lax.broadcasted_iota(jnp.int32, (GROUP, LANES), 0)
    keep = lax.rem(lane, GROUP) == sub
    zero = jnp.zeros((GROUP, LANES), f32)
    top = sub == 0

    def step(m, first):
        far_copy(m).wait()
        products = []
        for j in range(4):
            position = m * 4 + j
            blocks = []
            for d in range(total):
                halves = [
                    jnp.where(
                        keep,
                        jnp.broadcast_to(rows32[side, d, pl.ds(position, 1), :], (GROUP, LANES)),
                        zero,
                    )
                    for side in range(2)
                ]
                blocks.append(jnp.concatenate(halves, axis=1))
            left = jnp.concatenate(blocks, axis=0).astype(bf16)
            weight = jnp.concatenate([near_ref[position], far_ref[position]], axis=0)
            products.append(jnp.dot(left, weight, preferred_element_type=f32))
        base = pl.multiple_of(m * 16, 16)
        for d in range(total):
            a0, a1, b0, b1 = [p[d * GROUP : (d + 1) * GROUP] for p in products]
            s0, s1, t0, t1 = a0 + b0, a1 + b1, a0 - b0, a1 - b1
            even_real, odd_real = s0[:, :LANES], t0[:, :LANES]
            even_imag, odd_imag = t0[:, LANES:], s0[:, LANES:]
            if first:
                even_real = jnp.where(top, a0[:, :LANES], even_real)
                odd_real = jnp.where(top, a0[:, :LANES], odd_real)
                even_imag = jnp.where(top, b0[:, :LANES], even_imag)
                odd_imag = jnp.where(top, b0[:, LANES:], odd_imag)
            p, lanes = d // 2, pl.ds((d % 2) * LANES, LANES)
            for parity, offset, low, high in (
                (0, 0, even_real, s1[:, :LANES]),
                (0, HALF, even_imag, t1[:, LANES:]),
                (1, 0, odd_real, t1[:, :LANES]),
                (1, HALF, odd_imag, s1[:, LANES:]),
            ):
                cross[parity, p, pl.ds(base + offset, 16), lanes] = jnp.concatenate(
                    [low, high], axis=0
                ).astype(bf16)

    step(0, True)
    lax.fori_loop(1, STEPS, lambda m, c: (step(m, False), c)[1], 0)

    lag_copy.wait()
    targets = [(part[0], part[1] + i) for part in parts for i in range(part[2])]
    out_copies = []
    for p in range(pairs):
        for parity in range(2):
            lagged = jnp.dot(lag_ref[parity], cross[parity, p], preferred_element_type=f32)
            for d in range(2):
                mixed[p % 2, d, pl.ds(parity, LAGS // 2, stride=2), :] = lagged[:, d * LANES : (d + 1) * LANES]
        for d in range(2):
            result[2 * p + d] = jnp.transpose(mixed[p % 2, d].astype(bf16))[:row_count]
            target = targets[2 * p + d]
            copy = pltpu.make_async_copy(
                result.at[2 * p + d], out_ref.at[target[0], target[1]], out_sem.at[2 * p + d]
            )
            copy.start()
            out_copies.append(copy)
    for copy in out_copies:
        copy.wait()


def cross_part(near, far, lag_table, parts, sources, prior, local_rows, row_count):
    total = sum(part[2] for part in parts)
    any_space = pl.BlockSpec(memory_space=pl.ANY)
    operands = [near, far, lag_table] + sources
    specs = [pl.BlockSpec(memory_space=pltpu.VMEM)]
    specs += [pl.BlockSpec(memory_space=pltpu.MemorySpace.HBM)] * (len(sources) + 2)
    aliases = {}
    if prior is not None:
        aliases = {len(operands): 0}
        operands.append(prior)
        specs.append(any_space)
    return pl.pallas_call(
        functools.partial(cross_kernel, tuple(parts), row_count, prior is not None),
        out_shape=jax.ShapeDtypeStruct((ROUNDS, local_rows, row_count, LAGS), bf16),
        in_specs=specs,
        out_specs=any_space,
        scratch_shapes=[
            pltpu.VMEM(far.shape, bf16),
            pltpu.VMEM(lag_table.shape, bf16),
            pltpu.VMEM((2, total, OCTETS, LANES), bf16),
            pltpu.VMEM((2, total, OCTETS, LANES), f32),
            pltpu.VMEM((2, total // 2, 2 * HALF, 2 * LANES), bf16),
            pltpu.VMEM((2, 2, LAGS, LANES), f32),
            pltpu.VMEM((total, row_count, LAGS), bf16),
            pltpu.SemaphoreType.DMA((len(parts), 2)),
            pltpu.SemaphoreType.DMA((STEPS,)),
            pltpu.SemaphoreType.DMA,
            pltpu.SemaphoreType.DMA((total,)),
        ],
        input_output_aliases=aliases,
        compiler_params=pltpu.CompilerParams(vmem_limit_bytes=32 << 20),
        cost_estimate=pl.CostEstimate(
            flops=total * 600_000_000 // 4, bytes_accessed=12 << 20, transcendentals=0
        ),
        name="cross",
    )(*operands)


def chunk_rows(local_rows):
    if sum(ROWS_PER_CHUNK) == local_rows:
        return ROWS_PER_CHUNK
    return (local_rows,)


def local(signal, valid_flags):
    row_count = signal.shape[0]
    span_windows = signal.shape[1] // WINDOW
    owner_count = lax.axis_size("tm")
    blocks = lax.axis_size("chan")
    local_rows = row_count // owner_count
    chunks = chunk_rows(local_rows)
    me = lax.axis_index("tm").astype(jnp.int32)
    odd = lax.rem(lax.axis_index("chan"), 2).astype(jnp.int32)

    flags = valid_flags.T
    table, taper = forward_rows(), taper_row()
    live = first_flags(flags.astype(f32), chunks[0], local_rows)
    pieces = list(first_spectra(me[None], signal, live, table, taper, chunks[0], local_rows))
    *more, give, near = spectra(me[None], signal, flags, table, taper, chunks, local_rows)
    pieces += more

    def back(hops, side):
        return [
            (b * owner_count + t, (b - hops) % blocks * owner_count + (t + side) % owner_count)
            for b in range(blocks)
            for t in range(owner_count)
        ]

    axes = ("chan", "tm")
    two_away = [lax.ppermute(x, axes, back(2, i % 2)) for i, x in enumerate(pieces)]
    other = [(t, 1 - t) for t in range(owner_count)]
    taken = lax.ppermute(give, "tm", other)
    far = lax.ppermute(near, "tm", other)
    swap = [(b, b - 1 if b % 2 else b + 1) for b in range(blocks)]

    lag_table = lag_rows(span_windows * owner_count)
    out = None
    starts = np.cumsum([0] + list(chunks))
    one_away = []
    for k in range(len(chunks) + 1):
        parts, sources = [], []
        if k < len(chunks):
            sent = two_away[2 * k : 2 * k + 2]
            load = payload(odd[None], pieces[2 * k], taken, *sent, int(starts[k]))
            one_away.append(lax.ppermute(load, "chan", swap))
            parts.append((1, int(starts[k]), chunks[k], 2))
            sources += sent
        if k > 0:
            parts.append((0, int(starts[k - 1]), chunks[k - 1], 1))
            sources.append(one_away[k - 1])
        out = cross_part(near, far, lag_table, parts, sources, out, local_rows, row_count)
    return out


def solution(mesh):
    return jax.shard_map(
        local,
        mesh=mesh,
        in_specs=(P(("group", "chan"), "tm"), P(("group", "chan"), "tm")),
        out_specs=P(None, "tm", ("group", "chan"), None),
        check_vma=False,
    )
```

```python
import functools

import jax
import jax.numpy as jnp
import numpy as np
from jax import lax
from jax.experimental import pallas as pl
from jax.experimental.pallas import tpu as pltpu
from jax.sharding import PartitionSpec as P

WINDOW = 1024
LAGS = 512
ROUNDS = 2

epsilon = 1e-06

BINS = WINDOW // 2
HALF = BINS // 2
LANES = 128
GROUP = 8
OCTETS = BINS // GROUP
STEPS = OCTETS // 4
ROWS_PER_CHUNK = (18, 18, 16)

f32 = jnp.float32
bf16 = jnp.bfloat16


def frequency_order():
    order = np.zeros((OCTETS, GROUP), np.int64)
    for m in range(STEPS):
        for j in range(4):
            base = 16 * m + 8 * (j % 2) + np.arange(GROUP)
            order[4 * m + j] = base if j < 2 else np.where(base == 0, HALF, BINS - base)
    return order


def forward_rows():
    order = frequency_order()
    sample = np.arange(WINDOW)
    phases = 2.0 * np.pi / WINDOW * (order[:, :, None] * sample[None, None, :] % WINDOW)
    rows = np.stack([np.cos(phases), -np.sin(phases)], axis=1)
    return jnp.asarray(rows.reshape(WINDOW, WINDOW).astype(np.float32)).astype(bf16)


def lag_rows(windows):
    frequency = np.arange(HALF)
    weight = np.where(frequency == 0, 1.0, 2.0) / (WINDOW * float(WINDOW * windows) ** 0.5)
    tables = []
    for parity in range(2):
        shift = np.arange(parity, LAGS, 2)[:, None] - LAGS // 2
        phases = 2.0 * np.pi / WINDOW * (frequency[None, :] * shift % WINDOW)
        real = weight * np.cos(phases)
        imag = -weight * np.sin(phases)
        middle = 2.0 * np.pi / WINDOW * (HALF * shift[:, 0] % WINDOW)
        imag[:, 0] = weight[1] * (np.cos(middle) if parity == 0 else -np.sin(middle))
        tables.append(np.concatenate([real, imag], axis=1))
    return jnp.asarray(np.stack(tables).astype(np.float32)).astype(bf16)


def taper_row():
    return (0.5 - 0.5 * np.cos(2.0 * np.pi * np.arange(WINDOW) / WINDOW)).astype(np.float32)[None]


def window_order(spans):
    return [w for start in range(2) for w in range(start, spans, 2)]


def table_copies(table_hbm, table, sem):
    return [
        pltpu.make_async_copy(
            table_hbm.at[pl.ds(g * 256, 256)], table.at[pl.ds(g * 256, 256)], sem.at[g]
        )
        for g in range(4)
    ]


def taper_rows(x, taper):
    mean_square = jnp.mean(x * x, axis=1, keepdims=True)
    return (x * lax.rsqrt(mean_square + epsilon) * taper).astype(bf16)


def transform(table, tap, g):
    return lax.dot_general(
        table[g * 256 : (g + 1) * 256, :],
        tap[...],
        (((1,), (1,)), ((), ())),
        preferred_element_type=f32,
    )


def first_kernel(
    rows, half, bounds, me_ref, signal_hbm, flags_ref, table_hbm, taper_ref,
    same_ref, cross_ref, signal, tap, table, rows32, live, in_sem, table_sem,
):
    spans = signal.shape[1] // WINDOW
    width = LANES // 2
    loads, held = [], 0
    for h, (low, high) in enumerate(bounds):
        copy = pltpu.make_async_copy(
            signal_hbm.at[pl.ds(low, high - low)], signal.at[pl.ds(held, high - low)], in_sem.at[h]
        )
        copy.start()
        loads.append(copy)
        held += high - low
    tables = table_copies(table_hbm, table, table_sem)
    for copy in tables:
        copy.start()
    flags = flags_ref[...].astype(f32)
    flags = jnp.concatenate(
        [flags[:, low:high] for low, high in bounds] + [jnp.zeros((spans, width - held), f32)], axis=1
    )
    for v in range(spans // 2):
        live[v : v + 1, :] = jnp.concatenate(
            [flags[2 * v : 2 * v + 1], flags[2 * v + 1 : 2 * v + 2]], axis=1
        )
    taper = taper_ref[...]
    tap[...] = jnp.zeros_like(tap)
    for copy in loads:
        copy.wait()
    for w in range(spans):
        x = signal[:, w * WINDOW : (w + 1) * WINDOW]
        tap[pl.ds(w * width, held), :] = taper_rows(x, taper)
    for g in range(4):
        tables[g].wait()
        result = transform(table, tap, g)
        for o in range(16):
            position = g * 16 + o
            plain = jnp.concatenate(
                [
                    result[o * 16 : o * 16 + 16, v * LANES : (v + 1) * LANES] * live[v : v + 1, :]
                    for v in range(spans // 2)
                ],
                axis=0,
            )
            flipped = jnp.transpose(plain)
            for c in range(0, held, 8):
                rows32[pl.ds(c * OCTETS + position, 8, stride=OCTETS), :] = jnp.concatenate(
                    [flipped[c : c + 8], flipped[width + c : width + c + 8]], axis=1
                )
    me = me_ref[0]
    places = (-bounds[0][0], bounds[0][1] - bounds[0][0] + half - bounds[1][0])
    for side, out in enumerate((same_ref, cross_ref)):
        place = jnp.where(me == side, places[0], places[1])
        block = rows32[pl.ds(pl.multiple_of(place * OCTETS, OCTETS), rows * OCTETS), :]
        out[...] = block.astype(bf16).reshape(rows, OCTETS, LANES)


def first_spectra(me, signal, flags, table, taper, rows, half):
    spans = signal.shape[1] // WINDOW
    bounds = []
    for h in range(2):
        bounds.append((h * half // 8 * 8, -(-(h * half + rows) // 8) * 8))
    held = sum(high - low for low, high in bounds)
    assert held <= LANES // 2
    vmem = pl.BlockSpec(memory_space=pltpu.VMEM)
    hbm = pl.BlockSpec(memory_space=pltpu.MemorySpace.HBM)
    return pl.pallas_call(
        functools.partial(first_kernel, rows, half, tuple(bounds)),
        out_shape=[jax.ShapeDtypeStruct((rows, OCTETS, LANES), bf16)] * 2,
        in_specs=[pl.BlockSpec(memory_space=pltpu.SMEM), hbm, vmem, hbm, vmem],
        out_specs=[vmem] * 2,
        scratch_shapes=[
            pltpu.VMEM((held, spans * WINDOW), f32),
            pltpu.VMEM((spans * LANES // 2, WINDOW), bf16),
            pltpu.VMEM((WINDOW, WINDOW), bf16),
            pltpu.VMEM((held * OCTETS, LANES), f32),
            pltpu.VMEM((spans // 2, LANES), f32),
            pltpu.SemaphoreType.DMA((2,)),
            pltpu.SemaphoreType.DMA((4,)),
        ],
        compiler_params=pltpu.CompilerParams(vmem_limit_bytes=62 << 20),
        cost_estimate=pl.CostEstimate(flops=WINDOW**3, bytes_accessed=6 << 20, transcendentals=0),
        name="first",
    )(me, signal, flags, table, taper)


def spectra_kernel(
    chunks, half, me_ref, signal_hbm, flags_ref, table_hbm, taper_ref, *refs
):
    count = 2 * len(chunks) - 2
    pieces, (give_hbm, own_hbm) = refs[:count], refs[count : count + 2]
    signal, tap, table, rows32, live, own, give, in_sem, table_sem, own_sem, give_sem = refs[count + 2 :]
    row_count = signal.shape[0]
    spans = signal.shape[1] // WINDOW
    loads = []
    for w in range(spans):
        part = pl.ds(w * WINDOW, WINDOW)
        copy = pltpu.make_async_copy(signal_hbm.at[:, part], signal.at[:, part], in_sem.at[w])
        copy.start()
        loads.append(copy)
    tables = table_copies(table_hbm, table, table_sem)
    for copy in tables:
        copy.start()
    taper = taper_ref[...]
    tap[...] = jnp.zeros_like(tap)
    live[...] = jnp.zeros_like(live)
    live[:, :row_count] = flags_ref[...].astype(f32)
    for w in range(spans):
        loads[w].wait()
        x = signal[:, w * WINDOW : (w + 1) * WINDOW]
        tap[pl.ds(w * LANES, row_count), :] = taper_rows(x, taper)
    order = window_order(spans)
    leaving = []
    for g in range(4):
        tables[g].wait()
        result = transform(table, tap, g)
        for o in range(16):
            position = g * 16 + o
            real, imag = [
                [
                    result[o * 16 + s * 8 : o * 16 + s * 8 + 8, w * LANES : (w + 1) * LANES]
                    * live[w : w + 1, :]
                    for w in order
                ]
                for s in range(2)
            ]
            plain = jnp.concatenate([p for pair in zip(real, imag) for p in pair], axis=0)
            turned = jnp.concatenate([p for r, i in zip(real, imag) for p in (i, -r)], axis=0)
            own[position, :, :LANES] = plain.astype(bf16)
            own[position, :, LANES:] = turned.astype(bf16)
            flipped = jnp.transpose(plain)
            for c in range(0, row_count, 8):
                rows32[pl.ds(c * OCTETS + position, 8, stride=OCTETS), :] = flipped[c : c + 8]
        part = pl.ds(g * 16, 16)
        leaving.append(pltpu.make_async_copy(own.at[part], own_hbm.at[part], own_sem.at[g]))
        leaving[-1].start()
    me = me_ref[0]

    def block(side, start, rows):
        first = (me * half if side == 0 else (1 - me) * half) + start
        value = rows32[pl.ds(pl.multiple_of(first * OCTETS, OCTETS), rows * OCTETS), :]
        return value.astype(bf16).reshape(rows, OCTETS, LANES)

    give[...] = block(1, 0, half)
    leaving.append(pltpu.make_async_copy(give, give_hbm, give_sem))
    leaving[-1].start()
    start = chunks[0]
    for k, rows in enumerate(chunks[1:]):
        for side in range(2):
            pieces[2 * k + side][...] = block(side, start, rows)
        start += rows
    for copy in leaving:
        copy.wait()


def spectra(me, signal, flags, table, taper, chunks, half):
    row_count = signal.shape[0]
    spans = signal.shape[1] // WINDOW
    shapes = [(rows, OCTETS, LANES) for rows in chunks[1:] for _ in range(2)]
    give, own = (half, OCTETS, LANES), (OCTETS, LANES, 2 * LANES)
    vmem = pl.BlockSpec(memory_space=pltpu.VMEM)
    hbm = pl.BlockSpec(memory_space=pltpu.MemorySpace.HBM)
    return pl.pallas_call(
        functools.partial(spectra_kernel, chunks, half),
        out_shape=[jax.ShapeDtypeStruct(shape, bf16) for shape in shapes + [give, own]],
        in_specs=[pl.BlockSpec(memory_space=pltpu.SMEM), hbm, vmem, hbm, vmem],
        out_specs=[vmem] * len(shapes) + [hbm] * 2,
        scratch_shapes=[
            pltpu.VMEM((row_count, spans * WINDOW), f32),
            pltpu.VMEM((spans * LANES, WINDOW), bf16),
            pltpu.VMEM((WINDOW, WINDOW), bf16),
            pltpu.VMEM((row_count * OCTETS, LANES), f32),
            pltpu.VMEM((spans, LANES), f32),
            pltpu.VMEM(own, bf16),
            pltpu.VMEM(give, bf16),
            pltpu.SemaphoreType.DMA((spans,)),
            pltpu.SemaphoreType.DMA((4,)),
            pltpu.SemaphoreType.DMA((4,)),
            pltpu.SemaphoreType.DMA,
        ],
        compiler_params=pltpu.CompilerParams(vmem_limit_bytes=62 << 20),
        cost_estimate=pl.CostEstimate(flops=2 * WINDOW**3, bytes_accessed=12 << 20, transcendentals=0),
        name="spectra",
    )(me, signal, flags, table, taper)


def join_kernel(near_hbm, far_hbm, out_ref, sem):
    copies = [
        pltpu.make_async_copy(side, out_ref.at[:, pl.ds(i * LANES, LANES), :], sem.at[i])
        for i, side in enumerate((near_hbm, far_hbm))
    ]
    for copy in copies:
        copy.start()
    for copy in copies:
        copy.wait()


def join(near, far):
    hbm = pl.BlockSpec(memory_space=pltpu.MemorySpace.HBM)
    return pl.pallas_call(
        join_kernel,
        out_shape=pltpu.VMEM((OCTETS, 2 * LANES, 2 * LANES), bf16),
        in_specs=[hbm] * 2,
        out_specs=pl.BlockSpec(memory_space=pltpu.VMEM),
        scratch_shapes=[pltpu.SemaphoreType.DMA((2,))],
        compiler_params=pltpu.CompilerParams(vmem_limit_bytes=48 << 20),
        cost_estimate=pl.CostEstimate(flops=0, bytes_accessed=17 << 20, transcendentals=0),
        name="join",
    )(near, far)


def payload_kernel(first, rows, odd_ref, keep, taken, near_side, far_side, out_ref, hold, in_sem, out_sem):
    odd = odd_ref[0]
    span = pl.ds(first, rows)
    own = [pltpu.make_async_copy(keep, hold.at[0], in_sem.at[0]),
           pltpu.make_async_copy(taken.at[span], hold.at[1], in_sem.at[1])]
    come = [pltpu.make_async_copy(near_side, hold.at[0], in_sem.at[0]),
            pltpu.make_async_copy(far_side, hold.at[1], in_sem.at[1])]
    for i in range(2):
        pl.when(odd != 0)(own[i].start)
        pl.when(odd == 0)(come[i].start)
    leave = [pltpu.make_async_copy(hold.at[i], out_ref.at[i], out_sem.at[i]) for i in range(2)]
    for i in range(2):
        come[i].wait()
        leave[i].start()
    for i in range(2):
        leave[i].wait()


def payload(odd, keep, taken, near_side, far_side, first):
    hbm = pl.BlockSpec(memory_space=pltpu.MemorySpace.HBM)
    shape = (2,) + keep.shape
    return pl.pallas_call(
        functools.partial(payload_kernel, first, keep.shape[0]),
        out_shape=jax.ShapeDtypeStruct(shape, bf16),
        in_specs=[pl.BlockSpec(memory_space=pltpu.SMEM)] + [hbm] * 4,
        out_specs=hbm,
        scratch_shapes=[
            pltpu.VMEM(shape, bf16),
            pltpu.SemaphoreType.DMA((2,)),
            pltpu.SemaphoreType.DMA((2,)),
        ],
        compiler_params=pltpu.CompilerParams(vmem_limit_bytes=48 << 20),
        cost_estimate=pl.CostEstimate(flops=0, bytes_accessed=2 << 20, transcendentals=0),
        name="payload",
    )(odd, keep, taken, near_side, far_side)


def cross_kernel(parts, row_count, has_prior, *refs):
    source_count = sum(part[3] for part in parts)
    weight_ref, lag_hbm = refs[:2]
    sources = refs[2 : 2 + source_count]
    rest = refs[2 + source_count + (1 if has_prior else 0) :]
    out_ref, lag_ref, packed, rows32, cross, mixed, result = rest[:7]
    in_sem, lag_sem, out_sem = rest[7:]
    total = sum(part[2] for part in parts)
    pairs = total // 2

    loads, cursor, row = [], 0, 0
    for index, (_, _, rows, arrays) in enumerate(parts):
        for side in range(2):
            source = sources[cursor].at[side] if arrays == 1 else sources[cursor + side]
            copy = pltpu.make_async_copy(
                source, packed.at[side, pl.ds(row, rows)], in_sem.at[index, side]
            )
            copy.start()
            loads.append((copy, side, row, rows))
        cursor += arrays
        row += rows

    lag_copy = pltpu.make_async_copy(lag_hbm, lag_ref, lag_sem)
    lag_copy.start()
    for copy, side, row, rows in loads:
        copy.wait()
        rows32[side, pl.ds(row, rows)] = packed[side, pl.ds(row, rows)].astype(f32)

    lane = lax.broadcasted_iota(jnp.int32, (GROUP, LANES), 1)
    sub = lax.broadcasted_iota(jnp.int32, (GROUP, LANES), 0)
    keep = lax.rem(lane, GROUP) == sub
    zero = jnp.zeros((GROUP, LANES), f32)
    top = sub == 0

    def step(m, first):
        products = []
        for j in range(4):
            position = m * 4 + j
            blocks = []
            for d in range(total):
                halves = [
                    jnp.where(
                        keep,
                        jnp.broadcast_to(rows32[side, d, pl.ds(position, 1), :], (GROUP, LANES)),
                        zero,
                    )
                    for side in range(2)
                ]
                blocks.append(jnp.concatenate(halves, axis=1))
            left = jnp.concatenate(blocks, axis=0).astype(bf16)
            weight = weight_ref[position]
            products.append(jnp.dot(left, weight, preferred_element_type=f32))
        base = pl.multiple_of(m * 16, 16)
        for d in range(total):
            a0, a1, b0, b1 = [p[d * GROUP : (d + 1) * GROUP] for p in products]
            s0, s1, t0, t1 = a0 + b0, a1 + b1, a0 - b0, a1 - b1
            even_real, odd_real = s0[:, :LANES], t0[:, :LANES]
            even_imag, odd_imag = t0[:, LANES:], s0[:, LANES:]
            if first:
                even_real = jnp.where(top, a0[:, :LANES], even_real)
                odd_real = jnp.where(top, a0[:, :LANES], odd_real)
                even_imag = jnp.where(top, b0[:, :LANES], even_imag)
                odd_imag = jnp.where(top, b0[:, LANES:], odd_imag)
            p, lanes = d // 2, pl.ds((d % 2) * LANES, LANES)
            for parity, offset, low, high in (
                (0, 0, even_real, s1[:, :LANES]),
                (0, HALF, even_imag, t1[:, LANES:]),
                (1, 0, odd_real, t1[:, :LANES]),
                (1, HALF, odd_imag, s1[:, LANES:]),
            ):
                cross[parity, p, pl.ds(base + offset, 16), lanes] = jnp.concatenate(
                    [low, high], axis=0
                ).astype(bf16)

    step(0, True)
    lax.fori_loop(1, STEPS, lambda m, c: (step(m, False), c)[1], 0)

    lag_copy.wait()
    targets = [(part[0], part[1] + i) for part in parts for i in range(part[2])]
    out_copies = []
    for p in range(pairs):
        for parity in range(2):
            lagged = jnp.dot(lag_ref[parity], cross[parity, p], preferred_element_type=f32)
            for d in range(2):
                mixed[p % 2, d, pl.ds(parity, LAGS // 2, stride=2), :] = lagged[:, d * LANES : (d + 1) * LANES]
        for d in range(2):
            result[2 * p + d] = jnp.transpose(mixed[p % 2, d].astype(bf16))[:row_count]
            target = targets[2 * p + d]
            copy = pltpu.make_async_copy(
                result.at[2 * p + d], out_ref.at[target[0], target[1]], out_sem.at[2 * p + d]
            )
            copy.start()
            out_copies.append(copy)
    for copy in out_copies:
        copy.wait()


def cross_part(weights, lag_table, parts, sources, prior, local_rows, row_count):
    total = sum(part[2] for part in parts)
    any_space = pl.BlockSpec(memory_space=pl.ANY)
    operands = [weights, lag_table] + sources
    specs = [pl.BlockSpec(memory_space=pltpu.VMEM)]
    specs += [pl.BlockSpec(memory_space=pltpu.MemorySpace.HBM)] * (len(sources) + 1)
    aliases = {}
    if prior is not None:
        aliases = {len(operands): 0}
        operands.append(prior)
        specs.append(any_space)
    return pl.pallas_call(
        functools.partial(cross_kernel, tuple(parts), row_count, prior is not None),
        out_shape=jax.ShapeDtypeStruct((ROUNDS, local_rows, row_count, LAGS), bf16),
        in_specs=specs,
        out_specs=any_space,
        scratch_shapes=[
            pltpu.VMEM(lag_table.shape, bf16),
            pltpu.VMEM((2, total, OCTETS, LANES), bf16),
            pltpu.VMEM((2, total, OCTETS, LANES), f32),
            pltpu.VMEM((2, total // 2, 2 * HALF, 2 * LANES), bf16),
            pltpu.VMEM((2, 2, LAGS, LANES), f32),
            pltpu.VMEM((total, row_count, LAGS), bf16),
            pltpu.SemaphoreType.DMA((len(parts), 2)),
            pltpu.SemaphoreType.DMA,
            pltpu.SemaphoreType.DMA((total,)),
        ],
        input_output_aliases=aliases,
        compiler_params=pltpu.CompilerParams(vmem_limit_bytes=32 << 20),
        cost_estimate=pl.CostEstimate(
            flops=total * 600_000_000 // 4, bytes_accessed=12 << 20, transcendentals=0
        ),
        name="cross",
    )(*operands)


def chunk_rows(local_rows):
    if sum(ROWS_PER_CHUNK) == local_rows:
        return ROWS_PER_CHUNK
    return (local_rows,)


def local(signal, valid_flags):
    row_count = signal.shape[0]
    span_windows = signal.shape[1] // WINDOW
    owner_count = lax.axis_size("tm")
    blocks = lax.axis_size("chan")
    local_rows = row_count // owner_count
    chunks = chunk_rows(local_rows)
    me = lax.axis_index("tm").astype(jnp.int32)
    odd = lax.rem(lax.axis_index("chan"), 2).astype(jnp.int32)

    flags = valid_flags.T
    table, taper = forward_rows(), taper_row()
    pieces = list(first_spectra(me[None], signal, flags, table, taper, chunks[0], local_rows))
    *more, give, near = spectra(me[None], signal, flags, table, taper, chunks, local_rows)
    pieces += more

    def back(hops, side):
        return [
            (b * owner_count + t, (b - hops) % blocks * owner_count + (t + side) % owner_count)
            for b in range(blocks)
            for t in range(owner_count)
        ]

    axes = ("chan", "tm")
    two_away = [lax.ppermute(x, axes, back(2, i % 2)) for i, x in enumerate(pieces)]
    other = [(t, 1 - t) for t in range(owner_count)]
    taken = lax.ppermute(give, "tm", other)
    far = lax.ppermute(near, "tm", other)
    weights = join(near, far)
    swap = [(b, b - 1 if b % 2 else b + 1) for b in range(blocks)]

    lag_table = lag_rows(span_windows * owner_count)
    out = None
    starts = np.cumsum([0] + list(chunks))
    one_away = []
    for k in range(len(chunks) + 1):
        parts, sources = [], []
        if k < len(chunks):
            sent = two_away[2 * k : 2 * k + 2]
            load = payload(odd[None], pieces[2 * k], taken, *sent, int(starts[k]))
            one_away.append(lax.ppermute(load, "chan", swap))
            parts.append((1, int(starts[k]), chunks[k], 2))
            sources += sent
        if k > 0:
            parts.append((0, int(starts[k - 1]), chunks[k - 1], 1))
            sources.append(one_away[k - 1])
        out = cross_part(weights, lag_table, parts, sources, out, local_rows, row_count)
    return out


def solution(mesh):
    return jax.shard_map(
        local,
        mesh=mesh,
        in_specs=(P(("group", "chan"), "tm"), P(("group", "chan"), "tm")),
        out_specs=P(None, "tm", ("group", "chan"), None),
        check_vma=False,
    )
```

```python
import functools

import jax
import jax.numpy as jnp
import numpy as np
from jax import lax
from jax.experimental import pallas as pl
from jax.experimental.pallas import tpu as pltpu
from jax.sharding import PartitionSpec as P

WINDOW = 1024
LAGS = 512
ROUNDS = 2

epsilon = 1e-06

BINS = WINDOW // 2
HALF = BINS // 2
LANES = 128
GROUP = 8
OCTETS = BINS // GROUP
STEPS = OCTETS // 4
ROWS_PER_CHUNK = (18, 18, 16)

f32 = jnp.float32
bf16 = jnp.bfloat16


def frequency_order():
    order = np.zeros((OCTETS, GROUP), np.int64)
    for m in range(STEPS):
        for j in range(4):
            base = 16 * m + 8 * (j % 2) + np.arange(GROUP)
            order[4 * m + j] = base if j < 2 else np.where(base == 0, HALF, BINS - base)
    return order


def forward_rows():
    order = frequency_order()
    sample = np.arange(WINDOW)
    phases = 2.0 * np.pi / WINDOW * (order[:, :, None] * sample[None, None, :] % WINDOW)
    rows = np.stack([np.cos(phases), -np.sin(phases)], axis=1)
    return jnp.asarray(rows.reshape(WINDOW, WINDOW).astype(np.float32)).astype(bf16)


def lag_rows(windows):
    frequency = np.arange(HALF)
    weight = np.where(frequency == 0, 1.0, 2.0) / (WINDOW * float(WINDOW * windows) ** 0.5)
    tables = []
    for parity in range(2):
        shift = np.arange(parity, LAGS, 2)[:, None] - LAGS // 2
        phases = 2.0 * np.pi / WINDOW * (frequency[None, :] * shift % WINDOW)
        real = weight * np.cos(phases)
        imag = -weight * np.sin(phases)
        middle = 2.0 * np.pi / WINDOW * (HALF * shift[:, 0] % WINDOW)
        imag[:, 0] = weight[1] * (np.cos(middle) if parity == 0 else -np.sin(middle))
        tables.append(np.concatenate([real, imag], axis=1))
    return jnp.asarray(np.stack(tables).astype(np.float32)).astype(bf16)


def taper_row():
    return (0.5 - 0.5 * np.cos(2.0 * np.pi * np.arange(WINDOW) / WINDOW)).astype(np.float32)[None]


def window_order(spans):
    return [w for start in range(2) for w in range(start, spans, 2)]


def table_copies(table_hbm, table, sem):
    return [
        pltpu.make_async_copy(
            table_hbm.at[pl.ds(g * 256, 256)], table.at[pl.ds(g * 256, 256)], sem.at[g]
        )
        for g in range(4)
    ]


def taper_rows(x, taper):
    mean_square = jnp.mean(x * x, axis=1, keepdims=True)
    return (x * lax.rsqrt(mean_square + epsilon) * taper).astype(bf16)


def transform(table, tap, g):
    return lax.dot_general(
        table[g * 256 : (g + 1) * 256, :],
        tap[...],
        (((1,), (1,)), ((), ())),
        preferred_element_type=f32,
    )


def first_kernel(
    rows, half, bounds, me_ref, signal_hbm, flags_ref, table_hbm, taper_ref,
    same_ref, cross_ref, signal, tap, table, rows32, live, in_sem, table_sem,
):
    spans = signal.shape[1] // WINDOW
    width = LANES // 2
    loads, held = [], 0
    for h, (low, high) in enumerate(bounds):
        copy = pltpu.make_async_copy(
            signal_hbm.at[pl.ds(low, high - low)], signal.at[pl.ds(held, high - low)], in_sem.at[h]
        )
        copy.start()
        loads.append(copy)
        held += high - low
    tables = table_copies(table_hbm, table, table_sem)
    for copy in tables:
        copy.start()
    flags = flags_ref[...].astype(f32)
    flags = jnp.concatenate(
        [flags[:, low:high] for low, high in bounds] + [jnp.zeros((spans, width - held), f32)], axis=1
    )
    for v in range(spans // 2):
        live[v : v + 1, :] = jnp.concatenate(
            [flags[2 * v : 2 * v + 1], flags[2 * v + 1 : 2 * v + 2]], axis=1
        )
    taper = taper_ref[...]
    tap[...] = jnp.zeros_like(tap)
    for copy in loads:
        copy.wait()
    for w in range(spans):
        x = signal[:, w * WINDOW : (w + 1) * WINDOW]
        tap[pl.ds(w * width, held), :] = taper_rows(x, taper)
    for g in range(4):
        tables[g].wait()
        result = transform(table, tap, g)
        for o in range(16):
            position = g * 16 + o
            plain = jnp.concatenate(
                [
                    result[o * 16 : o * 16 + 16, v * LANES : (v + 1) * LANES] * live[v : v + 1, :]
                    for v in range(spans // 2)
                ],
                axis=0,
            )
            flipped = jnp.transpose(plain)
            for c in range(0, held, 8):
                rows32[pl.ds(c * OCTETS + position, 8, stride=OCTETS), :] = jnp.concatenate(
                    [flipped[c : c + 8], flipped[width + c : width + c + 8]], axis=1
                )
    me = me_ref[0]
    places = (-bounds[0][0], bounds[0][1] - bounds[0][0] + half - bounds[1][0])
    for side, out in enumerate((same_ref, cross_ref)):
        place = jnp.where(me == side, places[0], places[1])
        block = rows32[pl.ds(pl.multiple_of(place * OCTETS, OCTETS), rows * OCTETS), :]
        out[...] = block.astype(bf16).reshape(rows, OCTETS, LANES)


def first_spectra(me, signal, flags, table, taper, rows, half):
    spans = signal.shape[1] // WINDOW
    bounds = []
    for h in range(2):
        bounds.append((h * half // 8 * 8, -(-(h * half + rows) // 8) * 8))
    held = sum(high - low for low, high in bounds)
    assert held <= LANES // 2
    vmem = pl.BlockSpec(memory_space=pltpu.VMEM)
    hbm = pl.BlockSpec(memory_space=pltpu.MemorySpace.HBM)
    return pl.pallas_call(
        functools.partial(first_kernel, rows, half, tuple(bounds)),
        out_shape=[jax.ShapeDtypeStruct((rows, OCTETS, LANES), bf16)] * 2,
        in_specs=[pl.BlockSpec(memory_space=pltpu.SMEM), hbm, vmem, hbm, vmem],
        out_specs=[vmem] * 2,
        scratch_shapes=[
            pltpu.VMEM((held, spans * WINDOW), f32),
            pltpu.VMEM((spans * LANES // 2, WINDOW), bf16),
            pltpu.VMEM((WINDOW, WINDOW), bf16),
            pltpu.VMEM((held * OCTETS, LANES), f32),
            pltpu.VMEM((spans // 2, LANES), f32),
            pltpu.SemaphoreType.DMA((2,)),
            pltpu.SemaphoreType.DMA((4,)),
        ],
        compiler_params=pltpu.CompilerParams(vmem_limit_bytes=62 << 20),
        cost_estimate=pl.CostEstimate(flops=WINDOW**3, bytes_accessed=6 << 20, transcendentals=0),
        name="first",
    )(me, signal, flags, table, taper)


def spectra_kernel(
    chunks, half, me_ref, signal_hbm, flags_ref, table_hbm, taper_ref, *refs
):
    count = 2 * len(chunks) - 2
    pieces, (give_hbm, own_hbm) = refs[:count], refs[count : count + 2]
    signal, tap, table, rows32, live, own, give, in_sem, table_sem, own_sem, give_sem = refs[count + 2 :]
    row_count = signal.shape[0]
    spans = signal.shape[1] // WINDOW
    loads = []
    for w in range(spans):
        part = pl.ds(w * WINDOW, WINDOW)
        copy = pltpu.make_async_copy(signal_hbm.at[:, part], signal.at[:, part], in_sem.at[w])
        copy.start()
        loads.append(copy)
    tables = table_copies(table_hbm, table, table_sem)
    for copy in tables:
        copy.start()
    taper = taper_ref[...]
    tap[...] = jnp.zeros_like(tap)
    live[...] = jnp.zeros_like(live)
    live[:, :row_count] = flags_ref[...].astype(f32)
    for w in range(spans):
        loads[w].wait()
        x = signal[:, w * WINDOW : (w + 1) * WINDOW]
        tap[pl.ds(w * LANES, row_count), :] = taper_rows(x, taper)
    order = window_order(spans)
    leaving = []
    for g in range(4):
        tables[g].wait()
        result = transform(table, tap, g)
        for o in range(16):
            position = g * 16 + o
            real, imag = [
                [
                    result[o * 16 + s * 8 : o * 16 + s * 8 + 8, w * LANES : (w + 1) * LANES]
                    * live[w : w + 1, :]
                    for w in order
                ]
                for s in range(2)
            ]
            plain = jnp.concatenate([p for pair in zip(real, imag) for p in pair], axis=0)
            own[position] = plain.astype(bf16)
            flipped = jnp.transpose(plain)
            for c in range(0, row_count, 8):
                rows32[pl.ds(c * OCTETS + position, 8, stride=OCTETS), :] = flipped[c : c + 8]
        part = pl.ds(g * 16, 16)
        leaving.append(pltpu.make_async_copy(own.at[part], own_hbm.at[part], own_sem.at[g]))
        leaving[-1].start()
    me = me_ref[0]

    def block(side, start, rows):
        first = (me * half if side == 0 else (1 - me) * half) + start
        value = rows32[pl.ds(pl.multiple_of(first * OCTETS, OCTETS), rows * OCTETS), :]
        return value.astype(bf16).reshape(rows, OCTETS, LANES)

    give[...] = block(1, 0, half)
    leaving.append(pltpu.make_async_copy(give, give_hbm, give_sem))
    leaving[-1].start()
    start = chunks[0]
    for k, rows in enumerate(chunks[1:]):
        for side in range(2):
            pieces[2 * k + side][...] = block(side, start, rows)
        start += rows
    for copy in leaving:
        copy.wait()


def spectra(me, signal, flags, table, taper, chunks, half):
    row_count = signal.shape[0]
    spans = signal.shape[1] // WINDOW
    shapes = [(rows, OCTETS, LANES) for rows in chunks[1:] for _ in range(2)]
    give, own = (half, OCTETS, LANES), (OCTETS, LANES, LANES)
    vmem = pl.BlockSpec(memory_space=pltpu.VMEM)
    hbm = pl.BlockSpec(memory_space=pltpu.MemorySpace.HBM)
    return pl.pallas_call(
        functools.partial(spectra_kernel, chunks, half),
        out_shape=[jax.ShapeDtypeStruct(shape, bf16) for shape in shapes + [give, own]],
        in_specs=[pl.BlockSpec(memory_space=pltpu.SMEM), hbm, vmem, hbm, vmem],
        out_specs=[vmem] * len(shapes) + [hbm] * 2,
        scratch_shapes=[
            pltpu.VMEM((row_count, spans * WINDOW), f32),
            pltpu.VMEM((spans * LANES, WINDOW), bf16),
            pltpu.VMEM((WINDOW, WINDOW), bf16),
            pltpu.VMEM((row_count * OCTETS, LANES), f32),
            pltpu.VMEM((spans, LANES), f32),
            pltpu.VMEM(own, bf16),
            pltpu.VMEM(give, bf16),
            pltpu.SemaphoreType.DMA((spans,)),
            pltpu.SemaphoreType.DMA((4,)),
            pltpu.SemaphoreType.DMA((4,)),
            pltpu.SemaphoreType.DMA,
        ],
        compiler_params=pltpu.CompilerParams(vmem_limit_bytes=62 << 20),
        cost_estimate=pl.CostEstimate(flops=2 * WINDOW**3, bytes_accessed=12 << 20, transcendentals=0),
        name="spectra",
    )(me, signal, flags, table, taper)


def join_kernel(near_hbm, far_hbm, out_ref, held, sem):
    groups = sem.shape[1]
    per = OCTETS // groups

    def copies(g):
        part = pl.ds(g * per, per)
        return [
            pltpu.make_async_copy(side.at[part], held.at[i, part], sem.at[i, g])
            for i, side in enumerate((near_hbm, far_hbm))
        ]

    for g in range(groups):
        for copy in copies(g):
            copy.start()

    def group(g, carry):
        for copy in copies(g):
            copy.wait()
        for i in range(2):
            for n in range(per):
                value = held[i, g * per + n]
                wide = value.astype(f32)
                turned = []
                for r in range(0, LANES, 16):
                    turned += [wide[r + 8 : r + 16], -wide[r : r + 8]]
                rows = pl.ds(i * LANES, LANES)
                out_ref[g * per + n, rows, :LANES] = value
                out_ref[g * per + n, rows, LANES:] = jnp.concatenate(turned, axis=0).astype(bf16)
        return carry

    lax.fori_loop(0, groups, group, 0)


def join(near, far):
    hbm = pl.BlockSpec(memory_space=pltpu.MemorySpace.HBM)
    return pl.pallas_call(
        join_kernel,
        out_shape=pltpu.VMEM((OCTETS, 2 * LANES, 2 * LANES), bf16),
        in_specs=[hbm] * 2,
        out_specs=pl.BlockSpec(memory_space=pltpu.VMEM),
        scratch_shapes=[
            pltpu.VMEM((2,) + near.shape, bf16),
            pltpu.SemaphoreType.DMA((2, 8)),
        ],
        compiler_params=pltpu.CompilerParams(vmem_limit_bytes=48 << 20),
        cost_estimate=pl.CostEstimate(flops=0, bytes_accessed=13 << 20, transcendentals=0),
        name="join",
    )(near, far)


def payload_kernel(first, rows, odd_ref, keep, taken, near_side, far_side, out_ref, hold, in_sem, out_sem):
    odd = odd_ref[0]
    span = pl.ds(first, rows)
    own = [pltpu.make_async_copy(keep, hold.at[0], in_sem.at[0]),
           pltpu.make_async_copy(taken.at[span], hold.at[1], in_sem.at[1])]
    come = [pltpu.make_async_copy(near_side, hold.at[0], in_sem.at[0]),
            pltpu.make_async_copy(far_side, hold.at[1], in_sem.at[1])]
    for i in range(2):
        pl.when(odd != 0)(own[i].start)
        pl.when(odd == 0)(come[i].start)
    leave = [pltpu.make_async_copy(hold.at[i], out_ref.at[i], out_sem.at[i]) for i in range(2)]
    for i in range(2):
        come[i].wait()
        leave[i].start()
    for i in range(2):
        leave[i].wait()


def payload(odd, keep, taken, near_side, far_side, first):
    hbm = pl.BlockSpec(memory_space=pltpu.MemorySpace.HBM)
    shape = (2,) + keep.shape
    return pl.pallas_call(
        functools.partial(payload_kernel, first, keep.shape[0]),
        out_shape=jax.ShapeDtypeStruct(shape, bf16),
        in_specs=[pl.BlockSpec(memory_space=pltpu.SMEM)] + [hbm] * 4,
        out_specs=hbm,
        scratch_shapes=[
            pltpu.VMEM(shape, bf16),
            pltpu.SemaphoreType.DMA((2,)),
            pltpu.SemaphoreType.DMA((2,)),
        ],
        compiler_params=pltpu.CompilerParams(vmem_limit_bytes=48 << 20),
        cost_estimate=pl.CostEstimate(flops=0, bytes_accessed=2 << 20, transcendentals=0),
        name="payload",
    )(odd, keep, taken, near_side, far_side)


def cross_kernel(parts, row_count, has_prior, *refs):
    source_count = sum(part[3] for part in parts)
    weight_ref, lag_hbm = refs[:2]
    sources = refs[2 : 2 + source_count]
    rest = refs[2 + source_count + (1 if has_prior else 0) :]
    out_ref, lag_ref, packed, rows32, cross, mixed, result = rest[:7]
    in_sem, lag_sem, out_sem = rest[7:]
    total = sum(part[2] for part in parts)
    pairs = total // 2

    loads, cursor, row = [], 0, 0
    for index, (_, _, rows, arrays) in enumerate(parts):
        for side in range(2):
            source = sources[cursor].at[side] if arrays == 1 else sources[cursor + side]
            copy = pltpu.make_async_copy(
                source, packed.at[side, pl.ds(row, rows)], in_sem.at[index, side]
            )
            copy.start()
            loads.append((copy, side, row, rows))
        cursor += arrays
        row += rows

    lag_copy = pltpu.make_async_copy(lag_hbm, lag_ref, lag_sem)
    lag_copy.start()
    for copy, side, row, rows in loads:
        copy.wait()
        rows32[side, pl.ds(row, rows)] = packed[side, pl.ds(row, rows)].astype(f32)

    lane = lax.broadcasted_iota(jnp.int32, (GROUP, LANES), 1)
    sub = lax.broadcasted_iota(jnp.int32, (GROUP, LANES), 0)
    keep = lax.rem(lane, GROUP) == sub
    zero = jnp.zeros((GROUP, LANES), f32)
    top = sub == 0

    def step(m, first):
        products = []
        for j in range(4):
            position = m * 4 + j
            blocks = []
            for d in range(total):
                halves = [
                    jnp.where(
                        keep,
                        jnp.broadcast_to(rows32[side, d, pl.ds(position, 1), :], (GROUP, LANES)),
                        zero,
                    )
                    for side in range(2)
                ]
                blocks.append(jnp.concatenate(halves, axis=1))
            left = jnp.concatenate(blocks, axis=0).astype(bf16)
            weight = weight_ref[position]
            products.append(jnp.dot(left, weight, preferred_element_type=f32))
        base = pl.multiple_of(m * 16, 16)
        for d in range(total):
            a0, a1, b0, b1 = [p[d * GROUP : (d + 1) * GROUP] for p in products]
            s0, s1, t0, t1 = a0 + b0, a1 + b1, a0 - b0, a1 - b1
            even_real, odd_real = s0[:, :LANES], t0[:, :LANES]
            even_imag, odd_imag = t0[:, LANES:], s0[:, LANES:]
            if first:
                even_real = jnp.where(top, a0[:, :LANES], even_real)
                odd_real = jnp.where(top, a0[:, :LANES], odd_real)
                even_imag = jnp.where(top, b0[:, :LANES], even_imag)
                odd_imag = jnp.where(top, b0[:, LANES:], odd_imag)
            p, lanes = d // 2, pl.ds((d % 2) * LANES, LANES)
            for parity, offset, low, high in (
                (0, 0, even_real, s1[:, :LANES]),
                (0, HALF, even_imag, t1[:, LANES:]),
                (1, 0, odd_real, t1[:, :LANES]),
                (1, HALF, odd_imag, s1[:, LANES:]),
            ):
                cross[parity, p, pl.ds(base + offset, 16), lanes] = jnp.concatenate(
                    [low, high], axis=0
                ).astype(bf16)

    step(0, True)
    lax.fori_loop(1, STEPS, lambda m, c: (step(m, False), c)[1], 0)

    lag_copy.wait()
    targets = [(part[0], part[1] + i) for part in parts for i in range(part[2])]
    out_copies = []
    for p in range(pairs):
        for parity in range(2):
            lagged = jnp.dot(lag_ref[parity], cross[parity, p], preferred_element_type=f32)
            for d in range(2):
                mixed[p % 2, d, pl.ds(parity, LAGS // 2, stride=2), :] = lagged[:, d * LANES : (d + 1) * LANES]
        for d in range(2):
            result[2 * p + d] = jnp.transpose(mixed[p % 2, d].astype(bf16))[:row_count]
            target = targets[2 * p + d]
            copy = pltpu.make_async_copy(
                result.at[2 * p + d], out_ref.at[target[0], target[1]], out_sem.at[2 * p + d]
            )
            copy.start()
            out_copies.append(copy)
    for copy in out_copies:
        copy.wait()


def cross_part(weights, lag_table, parts, sources, prior, local_rows, row_count):
    total = sum(part[2] for part in parts)
    any_space = pl.BlockSpec(memory_space=pl.ANY)
    operands = [weights, lag_table] + sources
    specs = [pl.BlockSpec(memory_space=pltpu.VMEM)]
    specs += [pl.BlockSpec(memory_space=pltpu.MemorySpace.HBM)] * (len(sources) + 1)
    aliases = {}
    if prior is not None:
        aliases = {len(operands): 0}
        operands.append(prior)
        specs.append(any_space)
    return pl.pallas_call(
        functools.partial(cross_kernel, tuple(parts), row_count, prior is not None),
        out_shape=jax.ShapeDtypeStruct((ROUNDS, local_rows, row_count, LAGS), bf16),
        in_specs=specs,
        out_specs=any_space,
        scratch_shapes=[
            pltpu.VMEM(lag_table.shape, bf16),
            pltpu.VMEM((2, total, OCTETS, LANES), bf16),
            pltpu.VMEM((2, total, OCTETS, LANES), f32),
            pltpu.VMEM((2, total // 2, 2 * HALF, 2 * LANES), bf16),
            pltpu.VMEM((2, 2, LAGS, LANES), f32),
            pltpu.VMEM((total, row_count, LAGS), bf16),
            pltpu.SemaphoreType.DMA((len(parts), 2)),
            pltpu.SemaphoreType.DMA,
            pltpu.SemaphoreType.DMA((total,)),
        ],
        input_output_aliases=aliases,
        compiler_params=pltpu.CompilerParams(vmem_limit_bytes=32 << 20),
        cost_estimate=pl.CostEstimate(
            flops=total * 600_000_000 // 4, bytes_accessed=12 << 20, transcendentals=0
        ),
        name="cross",
    )(*operands)


def chunk_rows(local_rows):
    if sum(ROWS_PER_CHUNK) == local_rows:
        return ROWS_PER_CHUNK
    return (local_rows,)


def local(signal, valid_flags):
    row_count = signal.shape[0]
    span_windows = signal.shape[1] // WINDOW
    owner_count = lax.axis_size("tm")
    blocks = lax.axis_size("chan")
    local_rows = row_count // owner_count
    chunks = chunk_rows(local_rows)
    me = lax.axis_index("tm").astype(jnp.int32)
    odd = lax.rem(lax.axis_index("chan"), 2).astype(jnp.int32)

    flags = valid_flags.T
    table, taper = forward_rows(), taper_row()
    pieces = list(first_spectra(me[None], signal, flags, table, taper, chunks[0], local_rows))
    *more, give, near = spectra(me[None], signal, flags, table, taper, chunks, local_rows)
    pieces += more

    def back(hops, side):
        return [
            (b * owner_count + t, (b - hops) % blocks * owner_count + (t + side) % owner_count)
            for b in range(blocks)
            for t in range(owner_count)
        ]

    axes = ("chan", "tm")
    two_away = [lax.ppermute(x, axes, back(2, i % 2)) for i, x in enumerate(pieces)]
    other = [(t, 1 - t) for t in range(owner_count)]
    taken = lax.ppermute(give, "tm", other)
    far = lax.ppermute(near, "tm", other)
    weights = join(near, far)
    swap = [(b, b - 1 if b % 2 else b + 1) for b in range(blocks)]

    lag_table = lag_rows(span_windows * owner_count)
    out = None
    starts = np.cumsum([0] + list(chunks))
    one_away = []
    for k in range(len(chunks) + 1):
        parts, sources = [], []
        if k < len(chunks):
            sent = two_away[2 * k : 2 * k + 2]
            load = payload(odd[None], pieces[2 * k], taken, *sent, int(starts[k]))
            one_away.append(lax.ppermute(load, "chan", swap))
            parts.append((1, int(starts[k]), chunks[k], 2))
            sources += sent
        if k > 0:
            parts.append((0, int(starts[k - 1]), chunks[k - 1], 1))
            sources.append(one_away[k - 1])
        out = cross_part(weights, lag_table, parts, sources, out, local_rows, row_count)
    return out


def solution(mesh):
    return jax.shard_map(
        local,
        mesh=mesh,
        in_specs=(P(("group", "chan"), "tm"), P(("group", "chan"), "tm")),
        out_specs=P(None, "tm", ("group", "chan"), None),
        check_vma=False,
    )
```

```python
import functools

import jax
import jax.numpy as jnp
import numpy as np
from jax import lax
from jax.experimental import pallas as pl
from jax.experimental.pallas import tpu as pltpu
from jax.sharding import PartitionSpec as P

WINDOW = 1024
LAGS = 512
ROUNDS = 2

epsilon = 1e-06

BINS = WINDOW // 2
HALF = BINS // 2
LANES = 128
GROUP = 8
OCTETS = BINS // GROUP
STEPS = OCTETS // 4
ROWS_PER_CHUNK = (18, 18, 16)

f32 = jnp.float32
bf16 = jnp.bfloat16


def frequency_order():
    order = np.zeros((OCTETS, GROUP), np.int64)
    for m in range(STEPS):
        for j in range(4):
            base = 16 * m + 8 * (j % 2) + np.arange(GROUP)
            order[4 * m + j] = base if j < 2 else np.where(base == 0, HALF, BINS - base)
    return order


def forward_rows():
    order = frequency_order()
    sample = np.arange(WINDOW)
    phases = 2.0 * np.pi / WINDOW * (order[:, :, None] * sample[None, None, :] % WINDOW)
    rows = np.stack([np.cos(phases), -np.sin(phases)], axis=1)
    return jnp.asarray(rows.reshape(WINDOW, WINDOW).astype(np.float32)).astype(bf16)


def lag_rows(windows):
    frequency = np.arange(HALF)
    weight = np.where(frequency == 0, 1.0, 2.0) / (WINDOW * float(WINDOW * windows) ** 0.5)
    tables = []
    for parity in range(2):
        shift = np.arange(parity, LAGS, 2)[:, None] - LAGS // 2
        phases = 2.0 * np.pi / WINDOW * (frequency[None, :] * shift % WINDOW)
        real = weight * np.cos(phases)
        imag = -weight * np.sin(phases)
        middle = 2.0 * np.pi / WINDOW * (HALF * shift[:, 0] % WINDOW)
        imag[:, 0] = weight[1] * (np.cos(middle) if parity == 0 else -np.sin(middle))
        tables.append(np.concatenate([real, imag], axis=1))
    return jnp.asarray(np.stack(tables).astype(np.float32)).astype(bf16)


def taper_row():
    return (0.5 - 0.5 * np.cos(2.0 * np.pi * np.arange(WINDOW) / WINDOW)).astype(np.float32)[None]


def window_order(spans):
    return [w for start in range(2) for w in range(start, spans, 2)]


def table_copies(table_hbm, table, sem):
    return [
        pltpu.make_async_copy(
            table_hbm.at[pl.ds(g * 256, 256)], table.at[pl.ds(g * 256, 256)], sem.at[g]
        )
        for g in range(4)
    ]


def taper_rows(x, taper):
    mean_square = jnp.mean(x * x, axis=1, keepdims=True)
    return (x * lax.rsqrt(mean_square + epsilon) * taper).astype(bf16)


def transform(table, tap, g):
    return lax.dot_general(
        table[g * 256 : (g + 1) * 256, :],
        tap[...],
        (((1,), (1,)), ((), ())),
        preferred_element_type=f32,
    )


def first_kernel(
    rows, half, bounds, me_ref, signal_hbm, flags_ref, table_hbm, taper_ref,
    same_ref, cross_ref, signal, tap, table, rows32, live, in_sem, table_sem,
):
    spans = signal.shape[1] // WINDOW
    width = LANES // 2
    loads, held = [], 0
    for h, (low, high) in enumerate(bounds):
        copy = pltpu.make_async_copy(
            signal_hbm.at[pl.ds(low, high - low)], signal.at[pl.ds(held, high - low)], in_sem.at[h]
        )
        copy.start()
        loads.append(copy)
        held += high - low
    tables = table_copies(table_hbm, table, table_sem)
    for copy in tables:
        copy.start()
    flags = flags_ref[...].astype(f32)
    flags = jnp.concatenate(
        [flags[:, low:high] for low, high in bounds] + [jnp.zeros((spans, width - held), f32)], axis=1
    )
    for v in range(spans // 2):
        live[v : v + 1, :] = jnp.concatenate(
            [flags[2 * v : 2 * v + 1], flags[2 * v + 1 : 2 * v + 2]], axis=1
        )
    taper = taper_ref[...]
    for copy in loads:
        copy.wait()
    for w in range(spans):
        x = signal[:, w * WINDOW : (w + 1) * WINDOW]
        tap[pl.ds(w * width, held), :] = taper_rows(x, taper)
    for g in range(4):
        tables[g].wait()
        result = transform(table, tap, g)
        for o in range(16):
            position = g * 16 + o
            plain = jnp.concatenate(
                [
                    result[o * 16 : o * 16 + 16, v * LANES : (v + 1) * LANES] * live[v : v + 1, :]
                    for v in range(spans // 2)
                ],
                axis=0,
            )
            flipped = jnp.transpose(plain)
            for c in range(0, held, 8):
                rows32[pl.ds(c * OCTETS + position, 8, stride=OCTETS), :] = jnp.concatenate(
                    [flipped[c : c + 8], flipped[width + c : width + c + 8]], axis=1
                )
    me = me_ref[0]
    places = (-bounds[0][0], bounds[0][1] - bounds[0][0] + half - bounds[1][0])
    for side, out in enumerate((same_ref, cross_ref)):
        place = jnp.where(me == side, places[0], places[1])
        block = rows32[pl.ds(pl.multiple_of(place * OCTETS, OCTETS), rows * OCTETS), :]
        out[...] = block.astype(bf16).reshape(rows, OCTETS, LANES)


def first_spectra(me, signal, flags, table, taper, rows, half):
    spans = signal.shape[1] // WINDOW
    bounds = []
    for h in range(2):
        bounds.append((h * half // 8 * 8, -(-(h * half + rows) // 8) * 8))
    held = sum(high - low for low, high in bounds)
    assert held <= LANES // 2
    vmem = pl.BlockSpec(memory_space=pltpu.VMEM)
    hbm = pl.BlockSpec(memory_space=pltpu.MemorySpace.HBM)
    return pl.pallas_call(
        functools.partial(first_kernel, rows, half, tuple(bounds)),
        out_shape=[jax.ShapeDtypeStruct((rows, OCTETS, LANES), bf16)] * 2,
        in_specs=[pl.BlockSpec(memory_space=pltpu.SMEM), hbm, vmem, hbm, vmem],
        out_specs=[vmem] * 2,
        scratch_shapes=[
            pltpu.VMEM((held, spans * WINDOW), f32),
            pltpu.VMEM((spans * LANES // 2, WINDOW), bf16),
            pltpu.VMEM((WINDOW, WINDOW), bf16),
            pltpu.VMEM((held * OCTETS, LANES), f32),
            pltpu.VMEM((spans // 2, LANES), f32),
            pltpu.SemaphoreType.DMA((2,)),
            pltpu.SemaphoreType.DMA((4,)),
        ],
        compiler_params=pltpu.CompilerParams(vmem_limit_bytes=62 << 20),
        cost_estimate=pl.CostEstimate(flops=WINDOW**3, bytes_accessed=6 << 20, transcendentals=0),
        name="first",
    )(me, signal, flags, table, taper)


def spectra_kernel(
    chunks, half, me_ref, signal_hbm, flags_ref, table_hbm, taper_ref, *refs
):
    count = 2 * len(chunks) - 2
    pieces, own_hbm = refs[:count], refs[count]
    signal, tap, table, rows32, live, own, in_sem, table_sem, own_sem = refs[count + 1 :]
    row_count = signal.shape[0]
    spans = signal.shape[1] // WINDOW
    loads = []
    for w in range(spans):
        part = pl.ds(w * WINDOW, WINDOW)
        copy = pltpu.make_async_copy(signal_hbm.at[:, part], signal.at[:, part], in_sem.at[w])
        copy.start()
        loads.append(copy)
    tables = table_copies(table_hbm, table, table_sem)
    for copy in tables:
        copy.start()
    taper = taper_ref[...]
    live[...] = jnp.zeros_like(live)
    live[:, :row_count] = flags_ref[...].astype(f32)
    for w in range(spans):
        loads[w].wait()
        x = signal[:, w * WINDOW : (w + 1) * WINDOW]
        tap[pl.ds(w * LANES, row_count), :] = taper_rows(x, taper)
    order = window_order(spans)
    leaving = []
    for g in range(4):
        tables[g].wait()
        result = transform(table, tap, g)
        for o in range(16):
            position = g * 16 + o
            real, imag = [
                [
                    result[o * 16 + s * 8 : o * 16 + s * 8 + 8, w * LANES : (w + 1) * LANES]
                    * live[w : w + 1, :]
                    for w in order
                ]
                for s in range(2)
            ]
            plain = jnp.concatenate([p for pair in zip(real, imag) for p in pair], axis=0)
            own[position] = plain.astype(bf16)
            flipped = jnp.transpose(plain)
            for c in range(0, row_count, 8):
                rows32[pl.ds(c * OCTETS + position, 8, stride=OCTETS), :] = flipped[c : c + 8]
        part = pl.ds(g * 16, 16)
        leaving.append(pltpu.make_async_copy(own.at[part], own_hbm.at[part], own_sem.at[g]))
        leaving[-1].start()
    me = me_ref[0]

    def block(side, start, rows):
        first = (me * half if side == 0 else (1 - me) * half) + start
        value = rows32[pl.ds(pl.multiple_of(first * OCTETS, OCTETS), rows * OCTETS), :]
        return value.astype(bf16).reshape(rows, OCTETS, LANES)

    start = chunks[0]
    for k, rows in enumerate(chunks[1:]):
        for side in range(2):
            pieces[2 * k + side][...] = block(side, start, rows)
        start += rows
    for copy in leaving:
        copy.wait()


def spectra(me, signal, flags, table, taper, chunks, half):
    row_count = signal.shape[0]
    spans = signal.shape[1] // WINDOW
    shapes = [(rows, OCTETS, LANES) for rows in chunks[1:] for _ in range(2)]
    own = (OCTETS, LANES, LANES)
    vmem = pl.BlockSpec(memory_space=pltpu.VMEM)
    hbm = pl.BlockSpec(memory_space=pltpu.MemorySpace.HBM)
    return pl.pallas_call(
        functools.partial(spectra_kernel, chunks, half),
        out_shape=[jax.ShapeDtypeStruct(shape, bf16) for shape in shapes + [own]],
        in_specs=[pl.BlockSpec(memory_space=pltpu.SMEM), hbm, vmem, hbm, vmem],
        out_specs=[vmem] * len(shapes) + [hbm],
        scratch_shapes=[
            pltpu.VMEM((row_count, spans * WINDOW), f32),
            pltpu.VMEM((spans * LANES, WINDOW), bf16),
            pltpu.VMEM((WINDOW, WINDOW), bf16),
            pltpu.VMEM((row_count * OCTETS, LANES), f32),
            pltpu.VMEM((spans, LANES), f32),
            pltpu.VMEM(own, bf16),
            pltpu.SemaphoreType.DMA((spans,)),
            pltpu.SemaphoreType.DMA((4,)),
            pltpu.SemaphoreType.DMA((4,)),
        ],
        compiler_params=pltpu.CompilerParams(vmem_limit_bytes=62 << 20),
        cost_estimate=pl.CostEstimate(flops=2 * WINDOW**3, bytes_accessed=12 << 20, transcendentals=0),
        name="spectra",
    )(me, signal, flags, table, taper)


def join_kernel(near_hbm, far_hbm, out_ref, held, sem):
    groups = sem.shape[1]
    per = OCTETS // groups

    def copies(g):
        part = pl.ds(g * per, per)
        return [
            pltpu.make_async_copy(side.at[part], held.at[i, part], sem.at[i, g])
            for i, side in enumerate((near_hbm, far_hbm))
        ]

    for g in range(groups):
        for copy in copies(g):
            copy.start()

    def group(g, carry):
        for copy in copies(g):
            copy.wait()
        for i in range(2):
            for n in range(per):
                value = held[i, g * per + n]
                wide = value.astype(f32)
                turned = []
                for r in range(0, LANES, 16):
                    turned += [wide[r + 8 : r + 16], -wide[r : r + 8]]
                rows = pl.ds(i * LANES, LANES)
                out_ref[g * per + n, rows, :LANES] = value
                out_ref[g * per + n, rows, LANES:] = jnp.concatenate(turned, axis=0).astype(bf16)
        return carry

    lax.fori_loop(0, groups, group, 0)


def join(near, far):
    hbm = pl.BlockSpec(memory_space=pltpu.MemorySpace.HBM)
    return pl.pallas_call(
        join_kernel,
        out_shape=pltpu.VMEM((OCTETS, 2 * LANES, 2 * LANES), bf16),
        in_specs=[hbm] * 2,
        out_specs=pl.BlockSpec(memory_space=pltpu.VMEM),
        scratch_shapes=[
            pltpu.VMEM((2,) + near.shape, bf16),
            pltpu.SemaphoreType.DMA((2, 8)),
        ],
        compiler_params=pltpu.CompilerParams(vmem_limit_bytes=54 << 20),
        cost_estimate=pl.CostEstimate(flops=0, bytes_accessed=13 << 20, transcendentals=0),
        name="join",
    )(near, far)


def payload_kernel(odd_ref, keep, taken, near_side, far_side, out_ref, hold, in_sem, out_sem):
    odd = odd_ref[0]
    own = [pltpu.make_async_copy(keep, hold.at[0], in_sem.at[0]),
           pltpu.make_async_copy(taken, hold.at[1], in_sem.at[1])]
    come = [pltpu.make_async_copy(near_side, hold.at[0], in_sem.at[0]),
            pltpu.make_async_copy(far_side, hold.at[1], in_sem.at[1])]
    for i in range(2):
        pl.when(odd != 0)(own[i].start)
        pl.when(odd == 0)(come[i].start)
    leave = [pltpu.make_async_copy(hold.at[i], out_ref.at[i], out_sem.at[i]) for i in range(2)]
    for i in range(2):
        come[i].wait()
        leave[i].start()
    for i in range(2):
        leave[i].wait()


def payload(odd, keep, taken, near_side, far_side, grant):
    hbm = pl.BlockSpec(memory_space=pltpu.MemorySpace.HBM)
    shape = (2,) + keep.shape
    return pl.pallas_call(
        payload_kernel,
        out_shape=jax.ShapeDtypeStruct(shape, bf16),
        in_specs=[pl.BlockSpec(memory_space=pltpu.SMEM)] + [hbm] * 4,
        out_specs=hbm,
        scratch_shapes=[
            pltpu.VMEM(shape, bf16),
            pltpu.SemaphoreType.DMA((2,)),
            pltpu.SemaphoreType.DMA((2,)),
        ],
        compiler_params=pltpu.CompilerParams(vmem_limit_bytes=grant << 20),
        cost_estimate=pl.CostEstimate(flops=0, bytes_accessed=2 << 20, transcendentals=0),
        name="payload",
    )(odd, keep, taken, near_side, far_side)


def cross_kernel(parts, row_count, has_prior, *refs):
    source_count = sum(part[3] for part in parts)
    weight_ref, lag_hbm = refs[:2]
    sources = refs[2 : 2 + source_count]
    rest = refs[2 + source_count + (1 if has_prior else 0) :]
    out_ref, lag_ref, packed, rows32, cross, mixed, result = rest[:7]
    in_sem, lag_sem, out_sem = rest[7:]
    total = sum(part[2] for part in parts)
    pairs = total // 2

    loads, cursor, row = [], 0, 0
    for index, (_, _, rows, arrays) in enumerate(parts):
        for side in range(2):
            source = sources[cursor].at[side] if arrays == 1 else sources[cursor + side]
            copy = pltpu.make_async_copy(
                source, packed.at[side, pl.ds(row, rows)], in_sem.at[index, side]
            )
            copy.start()
            loads.append((copy, side, row, rows))
        cursor += arrays
        row += rows

    lag_copy = pltpu.make_async_copy(lag_hbm, lag_ref, lag_sem)
    lag_copy.start()
    for copy, side, row, rows in loads:
        copy.wait()
        rows32[side, pl.ds(row, rows)] = packed[side, pl.ds(row, rows)].astype(f32)

    lane = lax.broadcasted_iota(jnp.int32, (GROUP, LANES), 1)
    sub = lax.broadcasted_iota(jnp.int32, (GROUP, LANES), 0)
    keep = lax.rem(lane, GROUP) == sub
    zero = jnp.zeros((GROUP, LANES), f32)
    top = sub == 0

    def step(m, first):
        products = []
        for j in range(4):
            position = m * 4 + j
            blocks = []
            for d in range(total):
                halves = [
                    jnp.where(
                        keep,
                        jnp.broadcast_to(rows32[side, d, pl.ds(position, 1), :], (GROUP, LANES)),
                        zero,
                    )
                    for side in range(2)
                ]
                blocks.append(jnp.concatenate(halves, axis=1))
            left = jnp.concatenate(blocks, axis=0).astype(bf16)
            weight = weight_ref[position]
            products.append(jnp.dot(left, weight, preferred_element_type=f32))
        base = pl.multiple_of(m * 16, 16)
        for d in range(total):
            a0, a1, b0, b1 = [p[d * GROUP : (d + 1) * GROUP] for p in products]
            s0, s1, t0, t1 = a0 + b0, a1 + b1, a0 - b0, a1 - b1
            even_real, odd_real = s0[:, :LANES], t0[:, :LANES]
            even_imag, odd_imag = t0[:, LANES:], s0[:, LANES:]
            if first:
                even_real = jnp.where(top, a0[:, :LANES], even_real)
                odd_real = jnp.where(top, a0[:, :LANES], odd_real)
                even_imag = jnp.where(top, b0[:, :LANES], even_imag)
                odd_imag = jnp.where(top, b0[:, LANES:], odd_imag)
            p, lanes = d // 2, pl.ds((d % 2) * LANES, LANES)
            for parity, offset, low, high in (
                (0, 0, even_real, s1[:, :LANES]),
                (0, HALF, even_imag, t1[:, LANES:]),
                (1, 0, odd_real, t1[:, :LANES]),
                (1, HALF, odd_imag, s1[:, LANES:]),
            ):
                cross[parity, p, pl.ds(base + offset, 16), lanes] = jnp.concatenate(
                    [low, high], axis=0
                ).astype(bf16)

    step(0, True)
    lax.fori_loop(1, STEPS, lambda m, c: (step(m, False), c)[1], 0)

    lag_copy.wait()
    targets = [(part[0], part[1] + i) for part in parts for i in range(part[2])]
    out_copies = []
    for p in range(pairs):
        for parity in range(2):
            lagged = jnp.dot(lag_ref[parity], cross[parity, p], preferred_element_type=f32)
            for d in range(2):
                mixed[p % 2, d, pl.ds(parity, LAGS // 2, stride=2), :] = lagged[:, d * LANES : (d + 1) * LANES]
        for d in range(2):
            result[2 * p + d] = jnp.transpose(mixed[p % 2, d].astype(bf16))[:row_count]
            target = targets[2 * p + d]
            copy = pltpu.make_async_copy(
                result.at[2 * p + d], out_ref.at[target[0], target[1]], out_sem.at[2 * p + d]
            )
            copy.start()
            out_copies.append(copy)
    for copy in out_copies:
        copy.wait()


def cross_part(weights, lag_table, parts, sources, prior, local_rows, row_count):
    total = sum(part[2] for part in parts)
    any_space = pl.BlockSpec(memory_space=pl.ANY)
    operands = [weights, lag_table] + sources
    specs = [pl.BlockSpec(memory_space=pltpu.VMEM)]
    specs += [pl.BlockSpec(memory_space=pltpu.MemorySpace.HBM)] * (len(sources) + 1)
    aliases = {}
    if prior is not None:
        aliases = {len(operands): 0}
        operands.append(prior)
        specs.append(any_space)
    return pl.pallas_call(
        functools.partial(cross_kernel, tuple(parts), row_count, prior is not None),
        out_shape=jax.ShapeDtypeStruct((ROUNDS, local_rows, row_count, LAGS), bf16),
        in_specs=specs,
        out_specs=any_space,
        scratch_shapes=[
            pltpu.VMEM(lag_table.shape, bf16),
            pltpu.VMEM((2, total, OCTETS, LANES), bf16),
            pltpu.VMEM((2, total, OCTETS, LANES), f32),
            pltpu.VMEM((2, total // 2, 2 * HALF, 2 * LANES), bf16),
            pltpu.VMEM((2, 2, LAGS, LANES), f32),
            pltpu.VMEM((total, row_count, LAGS), bf16),
            pltpu.SemaphoreType.DMA((len(parts), 2)),
            pltpu.SemaphoreType.DMA,
            pltpu.SemaphoreType.DMA((total,)),
        ],
        input_output_aliases=aliases,
        compiler_params=pltpu.CompilerParams(vmem_limit_bytes=32 << 20),
        cost_estimate=pl.CostEstimate(
            flops=total * 600_000_000 // 4, bytes_accessed=12 << 20, transcendentals=0
        ),
        name="cross",
    )(*operands)


def chunk_rows(local_rows):
    if sum(ROWS_PER_CHUNK) == local_rows:
        return ROWS_PER_CHUNK
    return (local_rows,)


def local(signal, valid_flags):
    row_count = signal.shape[0]
    span_windows = signal.shape[1] // WINDOW
    owner_count = lax.axis_size("tm")
    blocks = lax.axis_size("chan")
    local_rows = row_count // owner_count
    chunks = chunk_rows(local_rows)
    me = lax.axis_index("tm").astype(jnp.int32)
    odd = lax.rem(lax.axis_index("chan"), 2).astype(jnp.int32)

    flags = valid_flags.T
    table, taper = forward_rows(), taper_row()
    pieces = list(first_spectra(me[None], signal, flags, table, taper, chunks[0], local_rows))
    *more, near = spectra(me[None], signal, flags, table, taper, chunks, local_rows)
    pieces += more

    def back(hops, side):
        return [
            (b * owner_count + t, (b - hops) % blocks * owner_count + (t + side) % owner_count)
            for b in range(blocks)
            for t in range(owner_count)
        ]

    axes = ("chan", "tm")
    two_away = [lax.ppermute(x, axes, back(2, i % 2)) for i, x in enumerate(pieces)]
    other = [(t, 1 - t) for t in range(owner_count)]
    taken = [lax.ppermute(x, "tm", other) for x in pieces[1::2]]
    far = lax.ppermute(near, "tm", other)
    weights = join(near, far)
    swap = [(b, b - 1 if b % 2 else b + 1) for b in range(blocks)]

    lag_table = lag_rows(span_windows * owner_count)
    out = None
    starts = np.cumsum([0] + list(chunks))
    one_away = []
    for k in range(len(chunks) + 1):
        parts, sources = [], []
        if k < len(chunks):
            sent = two_away[2 * k : 2 * k + 2]
            load = payload(odd[None], pieces[2 * k], taken[k], *sent, 52 if k else 60)
            one_away.append(lax.ppermute(load, "chan", swap))
            parts.append((1, int(starts[k]), chunks[k], 2))
            sources += sent
        if k > 0:
            parts.append((0, int(starts[k - 1]), chunks[k - 1], 1))
            sources.append(one_away[k - 1])
        out = cross_part(weights, lag_table, parts, sources, out, local_rows, row_count)
    return out


def solution(mesh):
    return jax.shard_map(
        local,
        mesh=mesh,
        in_specs=(P(("group", "chan"), "tm"), P(("group", "chan"), "tm")),
        out_specs=P(None, "tm", ("group", "chan"), None),
        check_vma=False,
    )
```

```python
import functools

import jax
import jax.numpy as jnp
import numpy as np
from jax import lax
from jax.experimental import pallas as pl
from jax.experimental.pallas import tpu as pltpu
from jax.sharding import PartitionSpec as P

WINDOW = 1024
LAGS = 512
ROUNDS = 2

epsilon = 1e-06

BINS = WINDOW // 2
HALF = BINS // 2
LANES = 128
GROUP = 8
OCTETS = BINS // GROUP
STEPS = OCTETS // 4
ROWS_PER_CHUNK = (18, 20, 14)

f32 = jnp.float32
bf16 = jnp.bfloat16


def frequency_order():
    order = np.zeros((OCTETS, GROUP), np.int64)
    for m in range(STEPS):
        for j in range(4):
            base = 16 * m + 8 * (j % 2) + np.arange(GROUP)
            order[4 * m + j] = base if j < 2 else np.where(base == 0, HALF, BINS - base)
    return order


def forward_rows():
    order = frequency_order()
    sample = np.arange(WINDOW)
    phases = 2.0 * np.pi / WINDOW * (order[:, :, None] * sample[None, None, :] % WINDOW)
    rows = np.stack([np.cos(phases), -np.sin(phases)], axis=1)
    return jnp.asarray(rows.reshape(WINDOW, WINDOW).astype(np.float32)).astype(bf16)


def lag_rows(windows):
    frequency = np.arange(HALF)
    weight = np.where(frequency == 0, 1.0, 2.0) / (WINDOW * float(WINDOW * windows) ** 0.5)
    tables = []
    for parity in range(2):
        shift = np.arange(parity, LAGS, 2)[:, None] - LAGS // 2
        phases = 2.0 * np.pi / WINDOW * (frequency[None, :] * shift % WINDOW)
        real = weight * np.cos(phases)
        imag = -weight * np.sin(phases)
        middle = 2.0 * np.pi / WINDOW * (HALF * shift[:, 0] % WINDOW)
        imag[:, 0] = weight[1] * (np.cos(middle) if parity == 0 else -np.sin(middle))
        tables.append(np.concatenate([real, imag], axis=1))
    return jnp.asarray(np.stack(tables).astype(np.float32)).astype(bf16)


def taper_row():
    return (0.5 - 0.5 * np.cos(2.0 * np.pi * np.arange(WINDOW) / WINDOW)).astype(np.float32)[None]


def window_order(spans):
    return [w for start in range(2) for w in range(start, spans, 2)]


def table_copies(table_hbm, table, sem):
    return [
        pltpu.make_async_copy(
            table_hbm.at[pl.ds(g * 256, 256)], table.at[pl.ds(g * 256, 256)], sem.at[g]
        )
        for g in range(4)
    ]


def taper_rows(x, taper):
    mean_square = jnp.mean(x * x, axis=1, keepdims=True)
    return (x * lax.rsqrt(mean_square + epsilon) * taper).astype(bf16)


def transform(table, tap, g):
    return lax.dot_general(
        table[g * 256 : (g + 1) * 256, :],
        tap[...],
        (((1,), (1,)), ((), ())),
        preferred_element_type=f32,
    )


def first_kernel(
    rows, half, bounds, me_ref, signal_hbm, flags_ref, table_hbm, taper_ref,
    same_ref, cross_ref, signal, tap, table, rows32, live, in_sem, table_sem,
):
    spans = signal.shape[1] // WINDOW
    width = LANES // 2
    loads, held = [], 0
    for h, (low, high) in enumerate(bounds):
        copy = pltpu.make_async_copy(
            signal_hbm.at[pl.ds(low, high - low)], signal.at[pl.ds(held, high - low)], in_sem.at[h]
        )
        copy.start()
        loads.append(copy)
        held += high - low
    tables = table_copies(table_hbm, table, table_sem)
    for copy in tables:
        copy.start()
    flags = flags_ref[...].astype(f32)
    flags = jnp.concatenate(
        [flags[:, low:high] for low, high in bounds] + [jnp.zeros((spans, width - held), f32)], axis=1
    )
    for v in range(spans // 2):
        live[v : v + 1, :] = jnp.concatenate(
            [flags[2 * v : 2 * v + 1], flags[2 * v + 1 : 2 * v + 2]], axis=1
        )
    taper = taper_ref[...]
    for copy in loads:
        copy.wait()
    for w in range(spans):
        x = signal[:, w * WINDOW : (w + 1) * WINDOW]
        tap[pl.ds(w * width, held), :] = taper_rows(x, taper)
    for copy in tables:
        copy.wait()
    for g in range(4):
        result = transform(table, tap, g)
        for o in range(16):
            position = g * 16 + o
            plain = jnp.concatenate(
                [
                    result[o * 16 : o * 16 + 16, v * LANES : (v + 1) * LANES] * live[v : v + 1, :]
                    for v in range(spans // 2)
                ],
                axis=0,
            )
            flipped = jnp.transpose(plain)
            for c in range(0, held, 8):
                rows32[pl.ds(c * OCTETS + position, 8, stride=OCTETS), :] = jnp.concatenate(
                    [flipped[c : c + 8], flipped[width + c : width + c + 8]], axis=1
                )
    me = me_ref[0]
    places = (-bounds[0][0], bounds[0][1] - bounds[0][0] + half - bounds[1][0])
    for side, out in enumerate((same_ref, cross_ref)):
        place = jnp.where(me == side, places[0], places[1])
        block = rows32[pl.ds(pl.multiple_of(place * OCTETS, OCTETS), rows * OCTETS), :]
        out[...] = block.astype(bf16).reshape(rows, OCTETS, LANES)


def first_spectra(me, signal, flags, table, taper, rows, half):
    spans = signal.shape[1] // WINDOW
    bounds = []
    for h in range(2):
        bounds.append((h * half // 8 * 8, -(-(h * half + rows) // 8) * 8))
    held = sum(high - low for low, high in bounds)
    assert held <= LANES // 2
    vmem = pl.BlockSpec(memory_space=pltpu.VMEM)
    hbm = pl.BlockSpec(memory_space=pltpu.MemorySpace.HBM)
    return pl.pallas_call(
        functools.partial(first_kernel, rows, half, tuple(bounds)),
        out_shape=[jax.ShapeDtypeStruct((rows, OCTETS, LANES), bf16)] * 2,
        in_specs=[pl.BlockSpec(memory_space=pltpu.SMEM), hbm, vmem, hbm, vmem],
        out_specs=[vmem] * 2,
        scratch_shapes=[
            pltpu.VMEM((held, spans * WINDOW), f32),
            pltpu.VMEM((spans * LANES // 2, WINDOW), bf16),
            pltpu.VMEM((WINDOW, WINDOW), bf16),
            pltpu.VMEM((held * OCTETS, LANES), f32),
            pltpu.VMEM((spans // 2, LANES), f32),
            pltpu.SemaphoreType.DMA((2,)),
            pltpu.SemaphoreType.DMA((4,)),
        ],
        compiler_params=pltpu.CompilerParams(vmem_limit_bytes=62 << 20),
        cost_estimate=pl.CostEstimate(flops=WINDOW**3, bytes_accessed=6 << 20, transcendentals=0),
        name="first",
    )(me, signal, flags, table, taper)


def spectra_kernel(
    chunks, half, me_ref, signal_hbm, flags_ref, table_hbm, taper_ref, *refs
):
    count = 2 * len(chunks) - 2
    pieces, own_hbm = refs[:count], refs[count]
    signal, tap, table, rows32, live, own, in_sem, table_sem, own_sem = refs[count + 1 :]
    row_count = signal.shape[0]
    spans = signal.shape[1] // WINDOW
    loads = []
    for w in range(spans):
        part = pl.ds(w * WINDOW, WINDOW)
        copy = pltpu.make_async_copy(signal_hbm.at[:, part], signal.at[:, part], in_sem.at[w])
        copy.start()
        loads.append(copy)
    tables = table_copies(table_hbm, table, table_sem)
    for copy in tables:
        copy.start()
    taper = taper_ref[...]
    live[...] = jnp.zeros_like(live)
    live[:, :row_count] = flags_ref[...].astype(f32)
    for w in range(spans):
        loads[w].wait()
        x = signal[:, w * WINDOW : (w + 1) * WINDOW]
        tap[pl.ds(w * LANES, row_count), :] = taper_rows(x, taper)
    order = window_order(spans)
    leaving = []
    for copy in tables:
        copy.wait()
    for g in range(4):
        result = transform(table, tap, g)
        for o in range(16):
            position = g * 16 + o
            real, imag = [
                [
                    result[o * 16 + s * 8 : o * 16 + s * 8 + 8, w * LANES : (w + 1) * LANES]
                    * live[w : w + 1, :]
                    for w in order
                ]
                for s in range(2)
            ]
            plain = jnp.concatenate([p for pair in zip(real, imag) for p in pair], axis=0)
            own[position] = plain.astype(bf16)
            flipped = jnp.transpose(plain)
            for c in range(0, row_count, 8):
                rows32[pl.ds(c * OCTETS + position, 8, stride=OCTETS), :] = flipped[c : c + 8]
        part = pl.ds(g * 16, 16)
        leaving.append(pltpu.make_async_copy(own.at[part], own_hbm.at[part], own_sem.at[g]))
        leaving[-1].start()
    me = me_ref[0]

    def block(side, start, rows):
        first = (me * half if side == 0 else (1 - me) * half) + start
        value = rows32[pl.ds(pl.multiple_of(first * OCTETS, OCTETS), rows * OCTETS), :]
        return value.astype(bf16).reshape(rows, OCTETS, LANES)

    start = chunks[0]
    for k, rows in enumerate(chunks[1:]):
        for side in range(2):
            pieces[2 * k + side][...] = block(side, start, rows)
        start += rows
    for copy in leaving:
        copy.wait()


def spectra(me, signal, flags, table, taper, chunks, half):
    row_count = signal.shape[0]
    spans = signal.shape[1] // WINDOW
    shapes = [(rows, OCTETS, LANES) for rows in chunks[1:] for _ in range(2)]
    own = (OCTETS, LANES, LANES)
    vmem = pl.BlockSpec(memory_space=pltpu.VMEM)
    hbm = pl.BlockSpec(memory_space=pltpu.MemorySpace.HBM)
    return pl.pallas_call(
        functools.partial(spectra_kernel, chunks, half),
        out_shape=[jax.ShapeDtypeStruct(shape, bf16) for shape in shapes + [own]],
        in_specs=[pl.BlockSpec(memory_space=pltpu.SMEM), hbm, vmem, hbm, vmem],
        out_specs=[vmem] * len(shapes) + [hbm],
        scratch_shapes=[
            pltpu.VMEM((row_count, spans * WINDOW), f32),
            pltpu.VMEM((spans * LANES, WINDOW), bf16),
            pltpu.VMEM((WINDOW, WINDOW), bf16),
            pltpu.VMEM((row_count * OCTETS, LANES), f32),
            pltpu.VMEM((spans, LANES), f32),
            pltpu.VMEM(own, bf16),
            pltpu.SemaphoreType.DMA((spans,)),
            pltpu.SemaphoreType.DMA((4,)),
            pltpu.SemaphoreType.DMA((4,)),
        ],
        compiler_params=pltpu.CompilerParams(vmem_limit_bytes=62 << 20),
        cost_estimate=pl.CostEstimate(flops=2 * WINDOW**3, bytes_accessed=12 << 20, transcendentals=0),
        name="spectra",
    )(me, signal, flags, table, taper)


def join_kernel(near_hbm, far_hbm, out_ref, held, sem):
    groups = sem.shape[1]
    per = OCTETS // groups

    def copies(g):
        part = pl.ds(g * per, per)
        return [
            pltpu.make_async_copy(side.at[part], held.at[i, part], sem.at[i, g])
            for i, side in enumerate((near_hbm, far_hbm))
        ]

    for g in range(groups):
        for copy in copies(g):
            copy.start()

    def group(g, carry):
        for copy in copies(g):
            copy.wait()
        for i in range(2):
            for n in range(per):
                value = held[i, g * per + n]
                wide = value.astype(f32)
                turned = []
                for r in range(0, LANES, 16):
                    turned += [wide[r + 8 : r + 16], -wide[r : r + 8]]
                rows = pl.ds(i * LANES, LANES)
                out_ref[g * per + n, rows, :LANES] = value
                out_ref[g * per + n, rows, LANES:] = jnp.concatenate(turned, axis=0).astype(bf16)
        return carry

    lax.fori_loop(0, groups, group, 0)


def join(near, far):
    hbm = pl.BlockSpec(memory_space=pltpu.MemorySpace.HBM)
    return pl.pallas_call(
        join_kernel,
        out_shape=pltpu.VMEM((OCTETS, 2 * LANES, 2 * LANES), bf16),
        in_specs=[hbm] * 2,
        out_specs=pl.BlockSpec(memory_space=pltpu.VMEM),
        scratch_shapes=[
            pltpu.VMEM((2,) + near.shape, bf16),
            pltpu.SemaphoreType.DMA((2, 8)),
        ],
        compiler_params=pltpu.CompilerParams(vmem_limit_bytes=54 << 20),
        cost_estimate=pl.CostEstimate(flops=0, bytes_accessed=13 << 20, transcendentals=0),
        name="join",
    )(near, far)


def payload_kernel(odd_ref, keep, taken, near_side, far_side, out_ref, hold, in_sem, out_sem):
    odd = odd_ref[0]
    own = [pltpu.make_async_copy(keep, hold.at[0], in_sem.at[0]),
           pltpu.make_async_copy(taken, hold.at[1], in_sem.at[1])]
    come = [pltpu.make_async_copy(near_side, hold.at[0], in_sem.at[0]),
            pltpu.make_async_copy(far_side, hold.at[1], in_sem.at[1])]
    for i in range(2):
        pl.when(odd != 0)(own[i].start)
        pl.when(odd == 0)(come[i].start)
    leave = [pltpu.make_async_copy(hold.at[i], out_ref.at[i], out_sem.at[i]) for i in range(2)]
    for i in range(2):
        come[i].wait()
        leave[i].start()
    for i in range(2):
        leave[i].wait()


def payload(odd, keep, taken, near_side, far_side):
    hbm = pl.BlockSpec(memory_space=pltpu.MemorySpace.HBM)
    shape = (2,) + keep.shape
    return pl.pallas_call(
        payload_kernel,
        out_shape=jax.ShapeDtypeStruct(shape, bf16),
        in_specs=[pl.BlockSpec(memory_space=pltpu.SMEM)] + [hbm] * 4,
        out_specs=hbm,
        scratch_shapes=[
            pltpu.VMEM(shape, bf16),
            pltpu.SemaphoreType.DMA((2,)),
            pltpu.SemaphoreType.DMA((2,)),
        ],
        compiler_params=pltpu.CompilerParams(vmem_limit_bytes=48 << 20),
        cost_estimate=pl.CostEstimate(flops=0, bytes_accessed=2 << 20, transcendentals=0),
        name="payload",
    )(odd, keep, taken, near_side, far_side)


def cross_kernel(parts, row_count, has_prior, *refs):
    source_count = sum(part[3] for part in parts)
    weight_ref, lag_hbm = refs[:2]
    sources = refs[2 : 2 + source_count]
    rest = refs[2 + source_count + (1 if has_prior else 0) :]
    out_ref, lag_ref, packed, rows32, cross, mixed, result = rest[:7]
    in_sem, lag_sem, out_sem = rest[7:]
    total = sum(part[2] for part in parts)
    pairs = total // 2

    loads, cursor, row = [], 0, 0
    for index, (_, _, rows, arrays) in enumerate(parts):
        for side in range(2):
            source = sources[cursor].at[side] if arrays == 1 else sources[cursor + side]
            copy = pltpu.make_async_copy(
                source, packed.at[side, pl.ds(row, rows)], in_sem.at[index, side]
            )
            copy.start()
            loads.append((copy, side, row, rows))
        cursor += arrays
        row += rows

    lag_copy = pltpu.make_async_copy(lag_hbm, lag_ref, lag_sem)
    lag_copy.start()
    for copy, side, row, rows in loads:
        copy.wait()
        rows32[side, pl.ds(row, rows)] = packed[side, pl.ds(row, rows)].astype(f32)

    lane = lax.broadcasted_iota(jnp.int32, (GROUP, LANES), 1)
    sub = lax.broadcasted_iota(jnp.int32, (GROUP, LANES), 0)
    keep = lax.rem(lane, GROUP) == sub
    zero = jnp.zeros((GROUP, LANES), f32)
    top = sub == 0

    def step(m, first):
        products = []
        for j in range(4):
            position = m * 4 + j
            blocks = []
            for d in range(total):
                halves = [
                    jnp.where(
                        keep,
                        jnp.broadcast_to(rows32[side, d, pl.ds(position, 1), :], (GROUP, LANES)),
                        zero,
                    )
                    for side in range(2)
                ]
                blocks.append(jnp.concatenate(halves, axis=1))
            left = jnp.concatenate(blocks, axis=0).astype(bf16)
            weight = weight_ref[position]
            products.append(jnp.dot(left, weight, preferred_element_type=f32))
        base = pl.multiple_of(m * 16, 16)
        for d in range(total):
            a0, a1, b0, b1 = [p[d * GROUP : (d + 1) * GROUP] for p in products]
            s0, s1, t0, t1 = a0 + b0, a1 + b1, a0 - b0, a1 - b1
            even_real, odd_real = s0[:, :LANES], t0[:, :LANES]
            even_imag, odd_imag = t0[:, LANES:], s0[:, LANES:]
            if first:
                even_real = jnp.where(top, a0[:, :LANES], even_real)
                odd_real = jnp.where(top, a0[:, :LANES], odd_real)
                even_imag = jnp.where(top, b0[:, :LANES], even_imag)
                odd_imag = jnp.where(top, b0[:, LANES:], odd_imag)
            p, lanes = d // 2, pl.ds((d % 2) * LANES, LANES)
            for parity, offset, low, high in (
                (0, 0, even_real, s1[:, :LANES]),
                (0, HALF, even_imag, t1[:, LANES:]),
                (1, 0, odd_real, t1[:, :LANES]),
                (1, HALF, odd_imag, s1[:, LANES:]),
            ):
                cross[parity, p, pl.ds(base + offset, 16), lanes] = jnp.concatenate(
                    [low, high], axis=0
                ).astype(bf16)

    step(0, True)
    lax.fori_loop(1, STEPS, lambda m, c: (step(m, False), c)[1], 0)

    lag_copy.wait()
    targets = [(part[0], part[1] + i) for part in parts for i in range(part[2])]
    out_copies = []
    for p in range(pairs):
        for parity in range(2):
            lagged = jnp.dot(lag_ref[parity], cross[parity, p], preferred_element_type=f32)
            for d in range(2):
                mixed[p % 2, d, pl.ds(parity, LAGS // 2, stride=2), :] = lagged[:, d * LANES : (d + 1) * LANES]
        for d in range(2):
            result[2 * p + d] = jnp.transpose(mixed[p % 2, d].astype(bf16))[:row_count]
            target = targets[2 * p + d]
            copy = pltpu.make_async_copy(
                result.at[2 * p + d], out_ref.at[target[0], target[1]], out_sem.at[2 * p + d]
            )
            copy.start()
            out_copies.append(copy)
    for copy in out_copies:
        copy.wait()


def cross_part(weights, lag_table, parts, sources, prior, local_rows, row_count):
    total = sum(part[2] for part in parts)
    any_space = pl.BlockSpec(memory_space=pl.ANY)
    operands = [weights, lag_table] + sources
    specs = [pl.BlockSpec(memory_space=pltpu.VMEM)]
    specs += [pl.BlockSpec(memory_space=pltpu.MemorySpace.HBM)] * (len(sources) + 1)
    aliases = {}
    if prior is not None:
        aliases = {len(operands): 0}
        operands.append(prior)
        specs.append(any_space)
    return pl.pallas_call(
        functools.partial(cross_kernel, tuple(parts), row_count, prior is not None),
        out_shape=jax.ShapeDtypeStruct((ROUNDS, local_rows, row_count, LAGS), bf16),
        in_specs=specs,
        out_specs=any_space,
        scratch_shapes=[
            pltpu.VMEM(lag_table.shape, bf16),
            pltpu.VMEM((2, total, OCTETS, LANES), bf16),
            pltpu.VMEM((2, total, OCTETS, LANES), f32),
            pltpu.VMEM((2, total // 2, 2 * HALF, 2 * LANES), bf16),
            pltpu.VMEM((2, 2, LAGS, LANES), f32),
            pltpu.VMEM((total, row_count, LAGS), bf16),
            pltpu.SemaphoreType.DMA((len(parts), 2)),
            pltpu.SemaphoreType.DMA,
            pltpu.SemaphoreType.DMA((total,)),
        ],
        input_output_aliases=aliases,
        compiler_params=pltpu.CompilerParams(vmem_limit_bytes=32 << 20),
        cost_estimate=pl.CostEstimate(
            flops=total * 600_000_000 // 4, bytes_accessed=12 << 20, transcendentals=0
        ),
        name="cross",
    )(*operands)


def chunk_rows(local_rows):
    if sum(ROWS_PER_CHUNK) == local_rows:
        return ROWS_PER_CHUNK
    return (local_rows,)


def local(signal, valid_flags):
    row_count = signal.shape[0]
    span_windows = signal.shape[1] // WINDOW
    owner_count = lax.axis_size("tm")
    blocks = lax.axis_size("chan")
    local_rows = row_count // owner_count
    chunks = chunk_rows(local_rows)
    me = lax.axis_index("tm").astype(jnp.int32)
    odd = lax.rem(lax.axis_index("chan"), 2).astype(jnp.int32)

    flags = valid_flags.T
    table, taper = forward_rows(), taper_row()
    pieces = list(first_spectra(me[None], signal, flags, table, taper, chunks[0], local_rows))
    *more, near = spectra(me[None], signal, flags, table, taper, chunks, local_rows)
    pieces += more

    def back(hops, side):
        return [
            (b * owner_count + t, (b - hops) % blocks * owner_count + (t + side) % owner_count)
            for b in range(blocks)
            for t in range(owner_count)
        ]

    axes = ("chan", "tm")
    two_away = [lax.ppermute(x, axes, back(2, i % 2)) for i, x in enumerate(pieces)]
    other = [(t, 1 - t) for t in range(owner_count)]
    taken = [lax.ppermute(x, "tm", other) for x in pieces[1::2]]
    far = lax.ppermute(near, "tm", other)
    weights = join(near, far)
    swap = [(b, b - 1 if b % 2 else b + 1) for b in range(blocks)]

    lag_table = lag_rows(span_windows * owner_count)
    out = None
    starts = np.cumsum([0] + list(chunks))
    one_away = []
    for k in range(len(chunks) + 1):
        parts, sources = [], []
        if k < len(chunks):
            sent = two_away[2 * k : 2 * k + 2]
            load = payload(odd[None], pieces[2 * k], taken[k], *sent)
            one_away.append(lax.ppermute(load, "chan", swap))
            parts.append((1, int(starts[k]), chunks[k], 2))
            sources += sent
        if k > 0:
            parts.append((0, int(starts[k - 1]), chunks[k - 1], 1))
            sources.append(one_away[k - 1])
        out = cross_part(weights, lag_table, parts, sources, out, local_rows, row_count)
    return out


def solution(mesh):
    return jax.shard_map(
        local,
        mesh=mesh,
        in_specs=(P(("group", "chan"), "tm"), P(("group", "chan"), "tm")),
        out_specs=P(None, "tm", ("group", "chan"), None),
        check_vma=False,
    )
```

```python
import functools

import jax
import jax.numpy as jnp
import numpy as np
from jax import lax
from jax.experimental import pallas as pl
from jax.experimental.pallas import tpu as pltpu
from jax.sharding import PartitionSpec as P

WINDOW = 1024
LAGS = 512
ROUNDS = 2

epsilon = 1e-06

BINS = WINDOW // 2
HALF = BINS // 2
LANES = 128
GROUP = 8
OCTETS = BINS // GROUP
STEPS = OCTETS // 4
ROWS_PER_CHUNK = (16, 12, 12, 12)

f32 = jnp.float32
bf16 = jnp.bfloat16


def frequency_order():
    order = np.zeros((OCTETS, GROUP), np.int64)
    for m in range(STEPS):
        for j in range(4):
            base = 16 * m + 8 * (j % 2) + np.arange(GROUP)
            order[4 * m + j] = base if j < 2 else np.where(base == 0, HALF, BINS - base)
    return order


def forward_rows():
    order = frequency_order()
    sample = np.arange(WINDOW)
    phases = 2.0 * np.pi / WINDOW * (order[:, :, None] * sample[None, None, :] % WINDOW)
    rows = np.stack([np.cos(phases), -np.sin(phases)], axis=1)
    return jnp.asarray(rows.reshape(WINDOW, WINDOW).astype(np.float32)).astype(bf16)


def lag_rows(windows):
    frequency = np.arange(HALF)
    weight = np.where(frequency == 0, 1.0, 2.0) / (WINDOW * float(WINDOW * windows) ** 0.5)
    tables = []
    for parity in range(2):
        shift = np.arange(parity, LAGS, 2)[:, None] - LAGS // 2
        phases = 2.0 * np.pi / WINDOW * (frequency[None, :] * shift % WINDOW)
        real = weight * np.cos(phases)
        imag = -weight * np.sin(phases)
        middle = 2.0 * np.pi / WINDOW * (HALF * shift[:, 0] % WINDOW)
        imag[:, 0] = weight[1] * (np.cos(middle) if parity == 0 else -np.sin(middle))
        tables.append(np.concatenate([real, imag], axis=1))
    return jnp.asarray(np.stack(tables).astype(np.float32)).astype(bf16)


def taper_row():
    return (0.5 - 0.5 * np.cos(2.0 * np.pi * np.arange(WINDOW) / WINDOW)).astype(np.float32)[None]


def window_order(spans):
    return [w for start in range(2) for w in range(start, spans, 2)]


def table_copies(table_hbm, table, sem):
    return [
        pltpu.make_async_copy(
            table_hbm.at[pl.ds(g * 256, 256)], table.at[pl.ds(g * 256, 256)], sem.at[g]
        )
        for g in range(4)
    ]


def taper_rows(x, taper):
    mean_square = jnp.mean(x * x, axis=1, keepdims=True)
    return (x * lax.rsqrt(mean_square + epsilon) * taper).astype(bf16)


def transform(table, tap, g):
    return lax.dot_general(
        table[g * 256 : (g + 1) * 256, :],
        tap[...],
        (((1,), (1,)), ((), ())),
        preferred_element_type=f32,
    )


def first_kernel(
    rows, half, bounds, me_ref, signal_hbm, flags_ref, table_hbm, taper_ref,
    same_ref, cross_ref, signal, tap, table, rows32, live, in_sem, table_sem,
):
    spans = signal.shape[1] // WINDOW
    width = LANES // 2
    loads, held = [], 0
    for h, (low, high) in enumerate(bounds):
        copy = pltpu.make_async_copy(
            signal_hbm.at[pl.ds(low, high - low)], signal.at[pl.ds(held, high - low)], in_sem.at[h]
        )
        copy.start()
        loads.append(copy)
        held += high - low
    tables = table_copies(table_hbm, table, table_sem)
    for copy in tables:
        copy.start()
    flags = flags_ref[...].astype(f32)
    flags = jnp.concatenate(
        [flags[:, low:high] for low, high in bounds] + [jnp.zeros((spans, width - held), f32)], axis=1
    )
    for v in range(spans // 2):
        live[v : v + 1, :] = jnp.concatenate(
            [flags[2 * v : 2 * v + 1], flags[2 * v + 1 : 2 * v + 2]], axis=1
        )
    taper = taper_ref[...]
    for copy in loads:
        copy.wait()
    for w in range(spans):
        x = signal[:, w * WINDOW : (w + 1) * WINDOW]
        tap[pl.ds(w * width, held), :] = taper_rows(x, taper)
    for copy in tables:
        copy.wait()
    for g in range(4):
        result = transform(table, tap, g)
        for o in range(16):
            position = g * 16 + o
            plain = jnp.concatenate(
                [
                    result[o * 16 : o * 16 + 16, v * LANES : (v + 1) * LANES] * live[v : v + 1, :]
                    for v in range(spans // 2)
                ],
                axis=0,
            )
            flipped = jnp.transpose(plain)
            for c in range(0, held, 8):
                rows32[pl.ds(c * OCTETS + position, 8, stride=OCTETS), :] = jnp.concatenate(
                    [flipped[c : c + 8], flipped[width + c : width + c + 8]], axis=1
                )
    me = me_ref[0]
    places = (-bounds[0][0], bounds[0][1] - bounds[0][0] + half - bounds[1][0])
    for side, out in enumerate((same_ref, cross_ref)):
        place = jnp.where(me == side, places[0], places[1])
        block = rows32[pl.ds(pl.multiple_of(place * OCTETS, OCTETS), rows * OCTETS), :]
        out[...] = block.astype(bf16).reshape(rows, OCTETS, LANES)


def first_spectra(me, signal, flags, table, taper, rows, half):
    spans = signal.shape[1] // WINDOW
    bounds = []
    for h in range(2):
        bounds.append((h * half // 8 * 8, -(-(h * half + rows) // 8) * 8))
    held = sum(high - low for low, high in bounds)
    assert held <= LANES // 2
    vmem = pl.BlockSpec(memory_space=pltpu.VMEM)
    hbm = pl.BlockSpec(memory_space=pltpu.MemorySpace.HBM)
    return pl.pallas_call(
        functools.partial(first_kernel, rows, half, tuple(bounds)),
        out_shape=[jax.ShapeDtypeStruct((rows, OCTETS, LANES), bf16)] * 2,
        in_specs=[pl.BlockSpec(memory_space=pltpu.SMEM), hbm, vmem, hbm, vmem],
        out_specs=[vmem] * 2,
        scratch_shapes=[
            pltpu.VMEM((held, spans * WINDOW), f32),
            pltpu.VMEM((spans * LANES // 2, WINDOW), bf16),
            pltpu.VMEM((WINDOW, WINDOW), bf16),
            pltpu.VMEM((held * OCTETS, LANES), f32),
            pltpu.VMEM((spans // 2, LANES), f32),
            pltpu.SemaphoreType.DMA((2,)),
            pltpu.SemaphoreType.DMA((4,)),
        ],
        compiler_params=pltpu.CompilerParams(vmem_limit_bytes=62 << 20),
        cost_estimate=pl.CostEstimate(flops=WINDOW**3, bytes_accessed=6 << 20, transcendentals=0),
        name="first",
    )(me, signal, flags, table, taper)


def spectra_kernel(
    chunks, half, me_ref, signal_hbm, flags_ref, table_hbm, taper_ref, *refs
):
    count = 2 * len(chunks) - 2
    pieces, own_hbm = refs[:count], refs[count]
    signal, tap, table, rows32, live, own, in_sem, table_sem, own_sem = refs[count + 1 :]
    row_count = signal.shape[0]
    spans = signal.shape[1] // WINDOW
    loads = []
    for w in range(spans):
        part = pl.ds(w * WINDOW, WINDOW)
        copy = pltpu.make_async_copy(signal_hbm.at[:, part], signal.at[:, part], in_sem.at[w])
        copy.start()
        loads.append(copy)
    tables = table_copies(table_hbm, table, table_sem)
    for copy in tables:
        copy.start()
    taper = taper_ref[...]
    live[...] = jnp.zeros_like(live)
    live[:, :row_count] = flags_ref[...].astype(f32)
    for w in range(spans):
        loads[w].wait()
        x = signal[:, w * WINDOW : (w + 1) * WINDOW]
        tap[pl.ds(w * LANES, row_count), :] = taper_rows(x, taper)
    order = window_order(spans)
    leaving = []
    for copy in tables:
        copy.wait()
    for g in range(4):
        result = transform(table, tap, g)
        for o in range(16):
            position = g * 16 + o
            real, imag = [
                [
                    result[o * 16 + s * 8 : o * 16 + s * 8 + 8, w * LANES : (w + 1) * LANES]
                    * live[w : w + 1, :]
                    for w in order
                ]
                for s in range(2)
            ]
            plain = jnp.concatenate([p for pair in zip(real, imag) for p in pair], axis=0)
            own[position] = plain.astype(bf16)
            flipped = jnp.transpose(plain)
            for c in range(0, row_count, 8):
                rows32[pl.ds(c * OCTETS + position, 8, stride=OCTETS), :] = flipped[c : c + 8]
        part = pl.ds(g * 16, 16)
        leaving.append(pltpu.make_async_copy(own.at[part], own_hbm.at[part], own_sem.at[g]))
        leaving[-1].start()
    me = me_ref[0]

    def block(side, start, rows):
        first = (me * half if side == 0 else (1 - me) * half) + start
        value = rows32[pl.ds(pl.multiple_of(first * OCTETS, OCTETS), rows * OCTETS), :]
        return value.astype(bf16).reshape(rows, OCTETS, LANES)

    start = chunks[0]
    for k, rows in enumerate(chunks[1:]):
        for side in range(2):
            pieces[2 * k + side][...] = block(side, start, rows)
        start += rows
    for copy in leaving:
        copy.wait()


def spectra(me, signal, flags, table, taper, chunks, half):
    row_count = signal.shape[0]
    spans = signal.shape[1] // WINDOW
    shapes = [(rows, OCTETS, LANES) for rows in chunks[1:] for _ in range(2)]
    own = (OCTETS, LANES, LANES)
    vmem = pl.BlockSpec(memory_space=pltpu.VMEM)
    hbm = pl.BlockSpec(memory_space=pltpu.MemorySpace.HBM)
    return pl.pallas_call(
        functools.partial(spectra_kernel, chunks, half),
        out_shape=[jax.ShapeDtypeStruct(shape, bf16) for shape in shapes + [own]],
        in_specs=[pl.BlockSpec(memory_space=pltpu.SMEM), hbm, vmem, hbm, vmem],
        out_specs=[vmem] * len(shapes) + [hbm],
        scratch_shapes=[
            pltpu.VMEM((row_count, spans * WINDOW), f32),
            pltpu.VMEM((spans * LANES, WINDOW), bf16),
            pltpu.VMEM((WINDOW, WINDOW), bf16),
            pltpu.VMEM((row_count * OCTETS, LANES), f32),
            pltpu.VMEM((spans, LANES), f32),
            pltpu.VMEM(own, bf16),
            pltpu.SemaphoreType.DMA((spans,)),
            pltpu.SemaphoreType.DMA((4,)),
            pltpu.SemaphoreType.DMA((4,)),
        ],
        compiler_params=pltpu.CompilerParams(vmem_limit_bytes=62 << 20),
        cost_estimate=pl.CostEstimate(flops=2 * WINDOW**3, bytes_accessed=12 << 20, transcendentals=0),
        name="spectra",
    )(me, signal, flags, table, taper)


def join_kernel(near_hbm, far_hbm, out_ref, held, sem):
    groups = sem.shape[1]
    per = OCTETS // groups

    def copies(g):
        part = pl.ds(g * per, per)
        return [
            pltpu.make_async_copy(side.at[part], held.at[i, part], sem.at[i, g])
            for i, side in enumerate((near_hbm, far_hbm))
        ]

    for g in range(groups):
        for copy in copies(g):
            copy.start()

    def group(g, carry):
        for copy in copies(g):
            copy.wait()
        for i in range(2):
            for n in range(per):
                value = held[i, g * per + n]
                wide = value.astype(f32)
                turned = []
                for r in range(0, LANES, 16):
                    turned += [wide[r + 8 : r + 16], -wide[r : r + 8]]
                rows = pl.ds(i * LANES, LANES)
                out_ref[g * per + n, rows, :LANES] = value
                out_ref[g * per + n, rows, LANES:] = jnp.concatenate(turned, axis=0).astype(bf16)
        return carry

    lax.fori_loop(0, groups, group, 0)


def join(near, far):
    hbm = pl.BlockSpec(memory_space=pltpu.MemorySpace.HBM)
    return pl.pallas_call(
        join_kernel,
        out_shape=pltpu.VMEM((OCTETS, 2 * LANES, 2 * LANES), bf16),
        in_specs=[hbm] * 2,
        out_specs=pl.BlockSpec(memory_space=pltpu.VMEM),
        scratch_shapes=[
            pltpu.VMEM((2,) + near.shape, bf16),
            pltpu.SemaphoreType.DMA((2, 8)),
        ],
        compiler_params=pltpu.CompilerParams(vmem_limit_bytes=51 << 20),
        cost_estimate=pl.CostEstimate(flops=0, bytes_accessed=13 << 20, transcendentals=0),
        name="join",
    )(near, far)


def payload_kernel(odd_ref, keep, taken, near_side, far_side, out_ref, hold, in_sem, out_sem):
    odd = odd_ref[0]
    own = [pltpu.make_async_copy(keep, hold.at[0], in_sem.at[0]),
           pltpu.make_async_copy(taken, hold.at[1], in_sem.at[1])]
    come = [pltpu.make_async_copy(near_side, hold.at[0], in_sem.at[0]),
            pltpu.make_async_copy(far_side, hold.at[1], in_sem.at[1])]
    for i in range(2):
        pl.when(odd != 0)(own[i].start)
        pl.when(odd == 0)(come[i].start)
    leave = [pltpu.make_async_copy(hold.at[i], out_ref.at[i], out_sem.at[i]) for i in range(2)]
    for i in range(2):
        come[i].wait()
        leave[i].start()
    for i in range(2):
        leave[i].wait()


def payload(odd, keep, taken, near_side, far_side):
    hbm = pl.BlockSpec(memory_space=pltpu.MemorySpace.HBM)
    shape = (2,) + keep.shape
    return pl.pallas_call(
        payload_kernel,
        out_shape=jax.ShapeDtypeStruct(shape, bf16),
        in_specs=[pl.BlockSpec(memory_space=pltpu.SMEM)] + [hbm] * 4,
        out_specs=hbm,
        scratch_shapes=[
            pltpu.VMEM(shape, bf16),
            pltpu.SemaphoreType.DMA((2,)),
            pltpu.SemaphoreType.DMA((2,)),
        ],
        compiler_params=pltpu.CompilerParams(vmem_limit_bytes=48 << 20),
        cost_estimate=pl.CostEstimate(flops=0, bytes_accessed=2 << 20, transcendentals=0),
        name="payload",
    )(odd, keep, taken, near_side, far_side)


def cross_kernel(parts, row_count, has_prior, *refs):
    source_count = sum(part[3] for part in parts)
    weight_ref, lag_hbm = refs[:2]
    sources = refs[2 : 2 + source_count]
    rest = refs[2 + source_count + (1 if has_prior else 0) :]
    out_ref, lag_ref, packed, rows32, cross, mixed, result = rest[:7]
    in_sem, lag_sem, out_sem = rest[7:]
    total = sum(part[2] for part in parts)
    pairs = total // 2

    loads, cursor, row = [], 0, 0
    for index, (_, _, rows, arrays) in enumerate(parts):
        for side in range(2):
            source = sources[cursor].at[side] if arrays == 1 else sources[cursor + side]
            copy = pltpu.make_async_copy(
                source, packed.at[side, pl.ds(row, rows)], in_sem.at[index, side]
            )
            copy.start()
            loads.append((copy, side, row, rows))
        cursor += arrays
        row += rows

    lag_copy = pltpu.make_async_copy(lag_hbm, lag_ref, lag_sem)
    lag_copy.start()
    for copy, side, row, rows in loads:
        copy.wait()
        rows32[side, pl.ds(row, rows)] = packed[side, pl.ds(row, rows)].astype(f32)

    lane = lax.broadcasted_iota(jnp.int32, (GROUP, LANES), 1)
    sub = lax.broadcasted_iota(jnp.int32, (GROUP, LANES), 0)
    keep = lax.rem(lane, GROUP) == sub
    zero = jnp.zeros((GROUP, LANES), f32)
    top = sub == 0

    def step(m, first):
        products = []
        for j in range(4):
            position = m * 4 + j
            blocks = []
            for d in range(total):
                halves = [
                    jnp.where(
                        keep,
                        jnp.broadcast_to(rows32[side, d, pl.ds(position, 1), :], (GROUP, LANES)),
                        zero,
                    )
                    for side in range(2)
                ]
                blocks.append(jnp.concatenate(halves, axis=1))
            left = jnp.concatenate(blocks, axis=0).astype(bf16)
            weight = weight_ref[position]
            products.append(jnp.dot(left, weight, preferred_element_type=f32))
        base = pl.multiple_of(m * 16, 16)
        for d in range(total):
            a0, a1, b0, b1 = [p[d * GROUP : (d + 1) * GROUP] for p in products]
            s0, s1, t0, t1 = a0 + b0, a1 + b1, a0 - b0, a1 - b1
            even_real, odd_real = s0[:, :LANES], t0[:, :LANES]
            even_imag, odd_imag = t0[:, LANES:], s0[:, LANES:]
            if first:
                even_real = jnp.where(top, a0[:, :LANES], even_real)
                odd_real = jnp.where(top, a0[:, :LANES], odd_real)
                even_imag = jnp.where(top, b0[:, :LANES], even_imag)
                odd_imag = jnp.where(top, b0[:, LANES:], odd_imag)
            p, lanes = d // 2, pl.ds((d % 2) * LANES, LANES)
            for parity, offset, low, high in (
                (0, 0, even_real, s1[:, :LANES]),
                (0, HALF, even_imag, t1[:, LANES:]),
                (1, 0, odd_real, t1[:, :LANES]),
                (1, HALF, odd_imag, s1[:, LANES:]),
            ):
                cross[parity, p, pl.ds(base + offset, 16), lanes] = jnp.concatenate(
                    [low, high], axis=0
                ).astype(bf16)

    step(0, True)
    lax.fori_loop(1, STEPS, lambda m, c: (step(m, False), c)[1], 0, unroll=5)

    lag_copy.wait()
    targets = [(part[0], part[1] + i) for part in parts for i in range(part[2])]
    out_copies = []
    for p in range(pairs):
        for parity in range(2):
            lagged = jnp.dot(lag_ref[parity], cross[parity, p], preferred_element_type=f32)
            for d in range(2):
                mixed[p % 2, d, pl.ds(parity, LAGS // 2, stride=2), :] = lagged[:, d * LANES : (d + 1) * LANES]
        for d in range(2):
            result[2 * p + d] = jnp.transpose(mixed[p % 2, d].astype(bf16))[:row_count]
            target = targets[2 * p + d]
            copy = pltpu.make_async_copy(
                result.at[2 * p + d], out_ref.at[target[0], target[1]], out_sem.at[2 * p + d]
            )
            copy.start()
            out_copies.append(copy)
    for copy in out_copies:
        copy.wait()


def cross_part(weights, lag_table, parts, sources, prior, local_rows, row_count):
    total = sum(part[2] for part in parts)
    any_space = pl.BlockSpec(memory_space=pl.ANY)
    operands = [weights, lag_table] + sources
    specs = [pl.BlockSpec(memory_space=pltpu.VMEM)]
    specs += [pl.BlockSpec(memory_space=pltpu.MemorySpace.HBM)] * (len(sources) + 1)
    aliases = {}
    if prior is not None:
        aliases = {len(operands): 0}
        operands.append(prior)
        specs.append(any_space)
    return pl.pallas_call(
        functools.partial(cross_kernel, tuple(parts), row_count, prior is not None),
        out_shape=jax.ShapeDtypeStruct((ROUNDS, local_rows, row_count, LAGS), bf16),
        in_specs=specs,
        out_specs=any_space,
        scratch_shapes=[
            pltpu.VMEM(lag_table.shape, bf16),
            pltpu.VMEM((2, total, OCTETS, LANES), bf16),
            pltpu.VMEM((2, total, OCTETS, LANES), f32),
            pltpu.VMEM((2, total // 2, 2 * HALF, 2 * LANES), bf16),
            pltpu.VMEM((2, 2, LAGS, LANES), f32),
            pltpu.VMEM((total, row_count, LAGS), bf16),
            pltpu.SemaphoreType.DMA((len(parts), 2)),
            pltpu.SemaphoreType.DMA,
            pltpu.SemaphoreType.DMA((total,)),
        ],
        input_output_aliases=aliases,
        compiler_params=pltpu.CompilerParams(vmem_limit_bytes=32 << 20),
        cost_estimate=pl.CostEstimate(
            flops=total * 600_000_000 // 4, bytes_accessed=12 << 20, transcendentals=0
        ),
        name="cross",
    )(*operands)


def chunk_rows(local_rows):
    if sum(ROWS_PER_CHUNK) == local_rows:
        return ROWS_PER_CHUNK
    return (local_rows,)


def local(signal, valid_flags):
    row_count = signal.shape[0]
    span_windows = signal.shape[1] // WINDOW
    owner_count = lax.axis_size("tm")
    blocks = lax.axis_size("chan")
    local_rows = row_count // owner_count
    chunks = chunk_rows(local_rows)
    me = lax.axis_index("tm").astype(jnp.int32)
    odd = lax.rem(lax.axis_index("chan"), 2).astype(jnp.int32)

    flags = valid_flags.T
    table, taper = forward_rows(), taper_row()
    pieces = list(first_spectra(me[None], signal, flags, table, taper, chunks[0], local_rows))
    *more, near = spectra(me[None], signal, flags, table, taper, chunks, local_rows)
    pieces += more

    def back(hops, side):
        return [
            (b * owner_count + t, (b - hops) % blocks * owner_count + (t + side) % owner_count)
            for b in range(blocks)
            for t in range(owner_count)
        ]

    axes = ("chan", "tm")
    two_away = [lax.ppermute(x, axes, back(2, i % 2)) for i, x in enumerate(pieces)]
    other = [(t, 1 - t) for t in range(owner_count)]
    taken = [lax.ppermute(x, "tm", other) for x in pieces[1::2]]
    far = lax.ppermute(near, "tm", other)
    weights = join(near, far)
    swap = [(b, b - 1 if b % 2 else b + 1) for b in range(blocks)]

    lag_table = lag_rows(span_windows * owner_count)
    out = None
    starts = np.cumsum([0] + list(chunks))
    one_away = []
    for k in range(len(chunks) + 1):
        parts, sources = [], []
        if k < len(chunks):
            sent = two_away[2 * k : 2 * k + 2]
            load = payload(odd[None], pieces[2 * k], taken[k], *sent)
            one_away.append(lax.ppermute(load, "chan", swap))
            parts.append((1, int(starts[k]), chunks[k], 2))
            sources += sent
        if k > 0:
            parts.append((0, int(starts[k - 1]), chunks[k - 1], 1))
            sources.append(one_away[k - 1])
        out = cross_part(weights, lag_table, parts, sources, out, local_rows, row_count)
    return out


def solution(mesh):
    return jax.shard_map(
        local,
        mesh=mesh,
        in_specs=(P(("group", "chan"), "tm"), P(("group", "chan"), "tm")),
        out_specs=P(None, "tm", ("group", "chan"), None),
        check_vma=False,
    )
```
